768 devices in a mesh: stream: 16 (over y_hi, x, core), cross: 48 (over z, y_lo).
Axes of the slice: x: 4, y: 8 (y_hi: 2, y_lo: 4; y = y_hi * 4 + y_lo), z: 12, core: 2. Of those that a mesh axis runs over, the one named last changes fastest.
Arguments:
- residual: bfloat16 [64, 384, 64, 128], P('stream', 'cross'), may hold values from -6 to 6
- approx_inverse: bfloat16 [16, 4608, 64, 256], P('stream', 'cross'), may hold values from -0.375 to 0.375
- pattern: int32 [16, 4608, 4], P('stream', 'cross'), may hold values from 0 to 95
- live_blocks: int32 [16, 48], P('stream', 'cross'), may hold values from 1 to 32, as said below
- block_aggregate: int32 [64, 384], P('stream', 'cross'), may hold values from 0 to 127
- coarse_inverse: float32 [512, 1536], P('stream', 'cross'), may hold values from -0.12 to 0.12
Outputs:
- correction: float32 [64, 384, 64, 128], P('stream', 'cross')
The draws below stay inside these ranges and needn't reach their ends.
Inputs may be any that keep to these rules, and one draw needn't show every extreme that they name: `pattern`: block numbers of the extended grid, numbered row by row. `live_blocks`: some subdomain is full in every draw.
All inputs are finite; a program needn't handle non-finite values.
Results may differ from the reference program's by a relative error of at most 0.0065.
Values may be sent and summed in bfloat16 or wider, within the bound.
No kernel may reach another device: no remote copies, remote signals or barrier semaphores. Data moves between devices by JAX's collectives and lax.ppermute only.
A program may use at most 64 MiB of HBM per device.

```python
import jax
import jax.numpy as jnp
from jax import lax

BLOCK = 64
CELLS = 16
K = 4
GS = 4
GC = 8
NRHS = 128
AGG_DEV = 8
NE = 96
NAG = 128
NSB = 64
NCB = 384
N_STREAM = 16
N_CROSS = 48


def draw_live_blocks(key, part):
    first, second = jax.random.split(jax.random.fold_in(key, 17))
    counts = jax.random.randint(first, (N_STREAM * N_CROSS,), 1, GS * GC + 1)
    chosen = jax.random.randint(second, (), 0, N_STREAM * N_CROSS)
    filled = jnp.where(jnp.arange(N_STREAM * N_CROSS) == chosen, GS * GC, counts)
    return filled.reshape(N_STREAM, N_CROSS).astype(jnp.int32)


def set_ends(array, key, smallest, top_value):
    index_at = [jax.random.randint(jax.random.fold_in(key, axis), (), 0, length) for axis, length in enumerate(array.shape)]
    widest = array.shape.index(max(array.shape))
    next_to = index_at[:widest] + [(index_at[widest] + 1) % array.shape[widest]] + index_at[widest + 1:]
    return array.at[tuple(index_at)].set(smallest).at[tuple(next_to)].set(top_value)


def levels(rng, dims, cuts, least, high):
    loudness = 1.0
    for dim, blocks in cuts:
        steps = jax.random.uniform(jax.random.fold_in(jax.random.fold_in(rng, 6), dim), (blocks,), jnp.float32, least / len(cuts), high / len(cuts))
        loudness = loudness * jnp.repeat(jnp.exp(steps), dims[dim] // blocks).reshape((-1,) + (1,) * (len(dims) - 1 - dim))
    return loudness


def noise(rng, extent, scale, bound, pieces=(), kind=jnp.bfloat16):
    factor_of = levels(rng, extent, pieces, -0.22, 0.18) if pieces else 1.0
    entries = jax.random.normal(rng, extent, jnp.float32) * scale * factor_of
    return jnp.minimum(jnp.maximum(entries, -bound), bound).astype(kind)


def setup_inputs(seed: int = 0) -> dict:
    keys = jax.random.split(jax.random.key(seed), 7)
    residual = noise(keys[0], (NSB, NCB, BLOCK, NRHS), 1.0, 6.0, ((0, 16), (1, 48)))
    approx_inverse = noise(keys[1], (N_STREAM, N_CROSS * NE, BLOCK, K * BLOCK), (K * BLOCK) ** -0.5, 0.375, ((0, 16), (1, 48)))
    pattern = set_ends(jax.random.randint(keys[2], (N_STREAM, N_CROSS * NE, K), 0, NE), jax.random.fold_in(keys[2], 1), 0, NE - 1).astype(jnp.int32)
    live_blocks = draw_live_blocks(jax.random.fold_in(keys[6], 71), 0)
    block_aggregate = set_ends(jax.random.randint(keys[4], (NSB, NCB), 0, NAG), jax.random.fold_in(keys[4], 1), 0, NAG - 1).astype(jnp.int32)
    coarse_inverse = noise(keys[5], (N_STREAM * AGG_DEV * 4, N_CROSS * AGG_DEV * 4), 0.02, 0.12, ((0, 16), (1, 48)), jnp.float32)
    return {"residual": residual, "approx_inverse": approx_inverse, "pattern": pattern, "live_blocks": live_blocks, "block_aggregate": block_aggregate, "coarse_inverse": coarse_inverse}


def reference(residual, approx_inverse, pattern, live_blocks, block_aggregate, coarse_inverse):
    nsb = residual.shape[0]
    ncb = residual.shape[1]
    row_local = jnp.arange(nsb) % GS
    col_local = jnp.arange(ncb) % GC
    local = row_local[:, None] * GC + col_local[None, :]
    counted = jnp.repeat(jnp.repeat(live_blocks, GS, axis=0), GC, axis=1)
    live = local < counted
    masked = jnp.where(live[:, :, None, None], residual, jnp.zeros((), jnp.bfloat16))
    padded = jnp.pad(masked, ((2, 2), (2, 2), (0, 0), (0, 0)))
    zero = jnp.zeros((), jnp.int32)

    def visit(index, total):
        index = jnp.asarray(index).astype(jnp.int32)
        sidx = index // N_CROSS
        cidx = index % N_CROSS
        start = (sidx * GS, cidx * GC, zero, zero)
        extended = lax.dynamic_slice(padded, start, (GS + 4, GC + 4, BLOCK, NRHS)).reshape(NE, BLOCK, NRHS)
        blocks = lax.dynamic_slice(approx_inverse, (sidx, cidx * NE, zero, zero), (1, NE, BLOCK, K * BLOCK))[0]
        links = lax.dynamic_slice(pattern, (sidx, cidx * NE, zero), (1, NE, K))[0]
        picked = extended[links].reshape(NE, K * BLOCK, NRHS)
        local_fix = jnp.einsum("nac,ncr->nar", blocks.astype(jnp.float32), picked.astype(jnp.float32),
                               precision=lax.Precision.HIGHEST).reshape(GS + 4, GC + 4, BLOCK, NRHS)
        rounded = lax.optimization_barrier(local_fix.astype(jnp.bfloat16)).astype(jnp.float32)
        here = lax.dynamic_slice(total, start, (GS + 4, GC + 4, BLOCK, NRHS))
        return lax.dynamic_update_slice(total, here + rounded, start)

    total = lax.fori_loop(0, N_STREAM * N_CROSS, visit, jnp.zeros(padded.shape, jnp.float32))
    fine = total[2:-2, 2:-2]
    per_block = masked.astype(jnp.float32).reshape(nsb, ncb, 4, CELLS, NRHS).sum(axis=3).reshape(nsb, ncb, 4 * NRHS)

    def group(cidx):
        cidx = cidx.astype(jnp.int32)
        sums = lax.dynamic_slice(per_block, (zero, cidx * GC, zero), (nsb, GC, 4 * NRHS)).reshape(nsb * GC, 4 * NRHS)
        labels = lax.dynamic_slice(block_aggregate, (zero, cidx * GC), (nsb, GC)).reshape(-1)
        onehot = (labels[:, None] == jnp.arange(NAG, dtype=jnp.int32)[None, :]).astype(jnp.float32)
        coarse_residual = jnp.dot(onehot.T, sums, precision=lax.Precision.HIGHEST)
        inverse = lax.dynamic_slice(coarse_inverse, (zero, cidx * AGG_DEV * 4), (N_STREAM * AGG_DEV * 4, AGG_DEV * 4))
        inverse = inverse.reshape(N_STREAM, AGG_DEV * 4, AGG_DEV * 4)
        coarse = jnp.einsum("sij,sjr->sir", inverse, coarse_residual.reshape(N_STREAM, AGG_DEV * 4, NRHS),
                            precision=lax.Precision.HIGHEST).reshape(NAG, 4 * NRHS)
        return jnp.dot(onehot, coarse, precision=lax.Precision.HIGHEST).reshape(nsb, GC, 4 * NRHS)

    prolonged = lax.map(group, jnp.arange(N_CROSS, dtype=jnp.int32))
    prolonged = jnp.transpose(prolonged, (1, 0, 2, 3)).reshape(nsb, ncb, 4, 1, NRHS)
    spread = jnp.broadcast_to(prolonged, (nsb, ncb, 4, CELLS, NRHS)).reshape(nsb, ncb, BLOCK, NRHS)
    return jnp.where(live[:, :, None, None], fine + spread, jnp.zeros((), jnp.float32))
```

```python
import jax
import jax.numpy as jnp
from jax import lax
from jax.experimental import pallas as pl
from jax.experimental.pallas import tpu as pltpu
from jax.sharding import PartitionSpec as P

BF16 = jnp.bfloat16
F32 = jnp.float32
MIB = 1 << 20
VMEM = pl.BlockSpec(memory_space=pltpu.VMEM)
SMEM = pl.BlockSpec(memory_space=pltpu.SMEM)
ANY = pl.BlockSpec(memory_space=pl.ANY)


def shift(values, axis, step):
    count = lax.axis_size(axis)
    pairs = [(i, i + step) for i in range(count) if 0 <= i + step < count]
    return lax.ppermute(values, axis, pairs)


def shaped(shape, dtype):
    return jax.ShapeDtypeStruct(shape, dtype)


def cost(flops, moved):
    return pl.CostEstimate(flops=flops, bytes_accessed=moved, transcendentals=0)


def mask_kernel(live_ref, residual_ref, top_ref, bottom_ref, left_ref, right_ref):
    rows, columns = residual_ref.shape[:2]
    half = rows // 2
    live = live_ref[0, 0]
    for i in range(rows):
        for j in range(columns):
            block = residual_ref[i, j]
            kept = jnp.where(i * columns + j < live, block, jnp.zeros_like(block))
            if i < half:
                top_ref[i, j] = kept
            else:
                bottom_ref[i - half, j] = kept
            if j < 2:
                left_ref[i, j] = kept
            if j >= columns - 2:
                right_ref[i, j - columns + 2] = kept


def mask_blocks(live, residual):
    rows, columns, width, sides = residual.shape
    wide = shaped((rows // 2, columns, width, sides), BF16)
    tall = shaped((rows, 2, width, sides), BF16)
    return pl.pallas_call(
        mask_kernel,
        out_shape=(wide, wide, tall, tall),
        in_specs=[SMEM, VMEM],
        out_specs=(VMEM,) * 4,
        cost_estimate=cost(0, 2 * residual.size * 2),
        compiler_params=pltpu.CompilerParams(vmem_limit_bytes=4 * MIB),
        name="mask_blocks",
    )(live, residual)


def labels_of(agg_ref, shape, axis):
    rows, columns = agg_ref.shape
    place = lax.broadcasted_iota(jnp.int32, shape, axis) // 4
    labels = jnp.zeros(shape, jnp.int32)
    for i in range(rows):
        for j in range(columns):
            labels = jnp.where(place == i * columns + j, agg_ref[i, j], labels)
    return labels


def partial_kernel(live_ref, agg_ref, residual_ref, out_ref):
    unknowns, sides = residual_ref.shape
    rows, columns = agg_ref.shape
    fields = rows * columns * 4
    cells = unknowns // fields
    owners, slot, _ = out_ref.shape
    row = lax.broadcasted_iota(jnp.int32, (fields, unknowns), 0)
    column = lax.broadcasted_iota(jnp.int32, (fields, unknowns), 1)
    picks = jnp.where((column // cells == row) & (row // 4 < live_ref[0, 0]), 1.0, 0.0)
    sums = jnp.dot(picks.astype(BF16), residual_ref[...], preferred_element_type=F32)
    labels = labels_of(agg_ref, (1, fields), 1)
    row = lax.broadcasted_iota(jnp.int32, (owners * slot, fields), 0)
    column = lax.broadcasted_iota(jnp.int32, (owners * slot, fields), 1)
    onehot = jnp.where((labels == row // 4) & (row % 4 == column % 4), 1.0, 0.0)
    total = jnp.dot(
        onehot, sums, precision=lax.Precision.HIGHEST, preferred_element_type=F32
    )
    out_ref[...] = total.astype(BF16).reshape(owners, slot, sides)


def partial_sums(live, agg, residual, owners, slot):
    sides = residual.shape[-1]
    flat = residual.reshape(-1, sides)
    return pl.pallas_call(
        partial_kernel,
        out_shape=shaped((owners, slot, sides), BF16),
        in_specs=[SMEM, SMEM, VMEM],
        out_specs=VMEM,
        cost_estimate=cost(2 * 128 * flat.size, 2 * flat.size),
        compiler_params=pltpu.CompilerParams(vmem_limit_bytes=6 * MIB),
        name="partial_sums",
    )(live, agg, flat)


def solve_kernel(parts_ref, inverse_ref, out_ref):
    owners = parts_ref.shape[0]
    total = parts_ref[0].astype(F32)
    for i in range(1, owners):
        total = total + parts_ref[i].astype(F32)
    coarse = jnp.dot(
        inverse_ref[...],
        total,
        precision=lax.Precision.HIGHEST,
        preferred_element_type=F32,
    ).astype(BF16)
    for i in range(owners):
        out_ref[i] = coarse


def coarse_solve(parts, inverse):
    return pl.pallas_call(
        solve_kernel,
        out_shape=shaped(parts.shape, BF16),
        in_specs=[VMEM, VMEM],
        out_specs=VMEM,
        cost_estimate=cost(2 * parts.shape[1] * parts.size, 4 * parts.size),
        compiler_params=pltpu.CompilerParams(vmem_limit_bytes=2 * MIB),
        name="coarse_solve",
    )(parts, inverse)


def corners_kernel(left_ref, right_ref, up_ref, down_ref):
    half = up_ref.shape[0]
    up_ref[:, :2] = left_ref[:half]
    up_ref[:, 2:] = right_ref[:half]
    down_ref[:, :2] = left_ref[half:]
    down_ref[:, 2:] = right_ref[half:]


def corners(left, right):
    rows, _, width, sides = left.shape
    piece = shaped((rows // 2, 4, width, sides), BF16)
    return pl.pallas_call(
        corners_kernel,
        out_shape=(piece, piece),
        in_specs=[VMEM, VMEM],
        out_specs=(VMEM, VMEM),
        cost_estimate=cost(0, 8 * left.size),
        compiler_params=pltpu.CompilerParams(vmem_limit_bytes=2 * MIB),
        name="corners",
    )(left, right)


def fix_kernel(
    pattern_ref,
    blocks_ref,
    above,
    below,
    top,
    bottom,
    left,
    right,
    corner_above,
    corner_below,
    up_main,
    down_main,
    up_corner,
    down_corner,
    side_left,
    side_right,
    center,
    grid_ref,
    fixes,
    in_sems,
    out_sems,
):
    step = pl.program_id(0)
    tall, wide = fixes.shape[:2]
    last = tall - 1
    columns = wide - 4
    half = (tall - 4) // 2
    inner, outer = pl.ds(2, columns), pl.ds(2 + columns, 2)
    first = pl.ds(0, 2)

    def moves_in():
        pieces = []
        for i in range(tall):
            if i < 2:
                row = (corner_above.at[i, first], above.at[i], corner_above.at[i, pl.ds(2, 2)])
            elif i < tall - 2:
                j = i - 2
                own = top.at[j] if j < half else bottom.at[j - half]
                row = (left.at[j], own, right.at[j])
            else:
                j = i - tall + 2
                row = (corner_below.at[j, first], below.at[j], corner_below.at[j, pl.ds(2, 2)])
            for piece, start, count in zip(row, (0, 2, 2 + columns), (2, columns, 2)):
                pieces.append((piece, pl.ds(i * wide + start, count)))
        return [
            pltpu.make_async_copy(piece, grid_ref.at[place], in_sems.at[i])
            for i, (piece, place) in enumerate(pieces)
        ]

    def moves_out(begin, end_at):
        own, end = pl.ds(2, tall - 4), pl.ds(tall - 2, 2)
        pieces = [
            (up_main, (first, inner)),
            (up_corner.at[:, pl.ds(0, 2)], (first, first)),
            (up_corner.at[:, pl.ds(2, 2)], (first, outer)),
            (side_left, (own, first)),
            (side_right, (own, outer)),
            (center, (own, inner)),
            (down_main, (end, inner)),
            (down_corner.at[:, pl.ds(0, 2)], (end, first)),
            (down_corner.at[:, pl.ds(2, 2)], (end, outer)),
        ]
        return [
            pltpu.make_async_copy(fixes.at[place], piece, out_sems.at[i])
            for i, (piece, place) in enumerate(pieces)
            if begin <= i < end_at
        ]

    @pl.when(step == 0)
    def _():
        copies = moves_in()
        for copy in copies:
            copy.start()
        for copy in copies:
            copy.wait()

    for j in range(wide):
        n = step * wide + j
        picked = jnp.concatenate([grid_ref[pattern_ref[k, n]] for k in range(4)], axis=0)
        fix = jnp.dot(blocks_ref[j], picked, preferred_element_type=F32)
        fixes[step, j] = fix.astype(BF16)

    @pl.when(step == 1)
    def _():
        for copy in moves_out(0, 3):
            copy.start()

    @pl.when(step == last - 2)
    def _():
        for copy in moves_out(3, 6):
            copy.start()

    @pl.when(step == last)
    def _():
        for copy in moves_out(6, 9):
            copy.start()
        for copy in moves_out(0, 9):
            copy.wait()


def local_fixes(pattern, blocks, pieces, rows, columns):
    count, width, depth = blocks.shape
    sides = pieces[0].shape[-1]
    tall, wide = rows + 4, columns + 4
    main = shaped((2, columns, width, sides), BF16)
    corner = shaped((2, 4, width, sides), BF16)
    side = shaped((rows, 2, width, sides), BF16)
    center = shaped((rows, columns, width, sides), BF16)
    return pl.pallas_call(
        fix_kernel,
        out_shape=(main, main, corner, corner, side, side, center),
        grid_spec=pltpu.PrefetchScalarGridSpec(
            num_scalar_prefetch=0,
            grid=(tall,),
            in_specs=[SMEM, pl.BlockSpec((wide, width, depth), lambda i: (i, 0, 0))]
            + [ANY] * 8,
            out_specs=[ANY] * 7,
            scratch_shapes=[
                pltpu.VMEM((count, width, sides), BF16),
                pltpu.VMEM((tall, wide, width, sides), BF16),
                pltpu.SemaphoreType.DMA((3 * tall,)),
                pltpu.SemaphoreType.DMA((9,)),
            ],
        ),
        cost_estimate=cost(2 * blocks.size * sides, 2 * blocks.size + 4 * count * width * sides),
        compiler_params=pltpu.CompilerParams(vmem_limit_bytes=8 * MIB),
        name="local_fixes",
    )(pattern, blocks, *pieces)


def fold_kernel(left_ref, right_ref, above_ref, below_ref, out_left, out_right):
    half = above_ref.shape[0]
    for i in range(2 * half):
        source = above_ref if i < half else below_ref
        for j in range(2):
            row = i % half
            out_left[i, j] = (
                left_ref[i, j].astype(F32) + source[row, j].astype(F32)
            ).astype(BF16)
            out_right[i, j] = (
                right_ref[i, j].astype(F32) + source[row, 2 + j].astype(F32)
            ).astype(BF16)


def fold_sides(left, right, above, below):
    return pl.pallas_call(
        fold_kernel,
        out_shape=(shaped(left.shape, BF16), shaped(left.shape, BF16)),
        in_specs=[VMEM] * 4,
        out_specs=(VMEM, VMEM),
        cost_estimate=cost(2 * left.size, 12 * left.size),
        compiler_params=pltpu.CompilerParams(vmem_limit_bytes=2 * MIB),
        name="fold_sides",
    )(left, right, above, below)


def join_kernel(
    live_ref,
    agg_ref,
    coarse_ref,
    center_ref,
    above_ref,
    below_ref,
    left_ref,
    right_ref,
    out_ref,
    spread,
):
    step = pl.program_id(0)
    rows, columns, width, sides = center_ref.shape
    cells = width // 4

    @pl.when(step == 0)
    def _():
        shape = (spread.shape[0], coarse_ref.shape[0])
        row = lax.broadcasted_iota(jnp.int32, shape, 0)
        column = lax.broadcasted_iota(jnp.int32, shape, 1)
        labels = labels_of(agg_ref, (shape[0], 1), 0)
        onehot = jnp.where((column // 4 == labels) & (column % 4 == row % 4), 1.0, 0.0)
        spread[...] = jnp.dot(
            onehot.astype(BF16), coarse_ref[...], preferred_element_type=F32
        )

    def half(base, source):
        for i in range(rows):
            for j in range(columns):
                block = base * columns + i * columns + j
                total = center_ref[i, j].astype(F32) + source[i, j].astype(F32)
                if j < 2:
                    total = total + left_ref[i, j].astype(F32)
                if j >= columns - 2:
                    total = total + right_ref[i, j - columns + 2].astype(F32)
                lifted = jnp.concatenate(
                    [
                        jnp.broadcast_to(spread[pl.ds(block * 4 + f, 1), :], (cells, sides))
                        for f in range(4)
                    ],
                    axis=0,
                )
                total = total + lifted
                out_ref[i, j] = jnp.where(
                    block < live_ref[0, 0], total, jnp.zeros_like(total)
                )

    @pl.when(step == 0)
    def _():
        half(0, above_ref)

    @pl.when(step == 1)
    def _():
        half(rows, below_ref)


def join(live, agg, coarse, center, above, below, left, right):
    rows, columns, width, sides = center.shape
    half = rows // 2
    whole = pl.BlockSpec((half, columns, width, sides), lambda i: (0, 0, 0, 0))
    moving = pl.BlockSpec((half, columns, width, sides), lambda i: (i, 0, 0, 0))
    thin = pl.BlockSpec((half, 2, width, sides), lambda i: (i, 0, 0, 0))
    flat = pl.BlockSpec(coarse.shape, lambda i: (0, 0))
    return pl.pallas_call(
        join_kernel,
        out_shape=shaped(center.shape, F32),
        grid_spec=pltpu.PrefetchScalarGridSpec(
            num_scalar_prefetch=0,
            grid=(2,),
            in_specs=[SMEM, SMEM, flat, moving, whole, whole, thin, thin],
            out_specs=moving,
            scratch_shapes=[pltpu.VMEM((rows * columns * 4, sides), F32)],
        ),
        cost_estimate=cost(8 * center.size, 10 * center.size),
        compiler_params=pltpu.CompilerParams(vmem_limit_bytes=10 * MIB),
        name="join",
    )(live, agg, coarse, center, above, below, left, right)


def body(residual, approx_inverse, pattern, live_blocks, block_aggregate, coarse_inverse):
    rows, columns, width, sides = residual.shape
    owners = lax.axis_size("stream")
    slot = coarse_inverse.shape[0]
    top, bottom, left, right = mask_blocks(live_blocks, residual)
    from_left = shift(right, "cross", 1)
    from_right = shift(left, "cross", -1)
    above = shift(bottom, "stream", 1)
    below = shift(top, "stream", -1)
    parts = partial_sums(live_blocks, block_aggregate, residual, owners, slot)
    corner_up, corner_down = corners(from_left, from_right)
    corner_above = shift(corner_down, "stream", 1)
    corner_below = shift(corner_up, "stream", -1)
    parts, _ = lax.optimization_barrier((parts, corner_up))
    parts = lax.all_to_all(parts, "stream", 0, 0)
    corner_above, parts = lax.optimization_barrier((corner_above, parts))
    pieces = (above, below, top, bottom, from_left, from_right, corner_above, corner_below)
    up_main, down_main, up_corner, down_corner, side_left, side_right, center = local_fixes(
        jnp.transpose(pattern[0]), approx_inverse[0], pieces, rows, columns
    )
    corner_above = shift(down_corner, "stream", 1)
    corner_below = shift(up_corner, "stream", -1)
    above = shift(down_main, "stream", 1)
    below = shift(up_main, "stream", -1)
    coarse = coarse_solve(parts, coarse_inverse)
    out_left, out_right = fold_sides(side_left, side_right, corner_above, corner_below)
    from_right = shift(out_left, "cross", -1)
    from_left = shift(out_right, "cross", 1)
    coarse, _ = lax.optimization_barrier((coarse, out_left))
    coarse = lax.all_to_all(coarse, "stream", 0, 0).reshape(owners * slot, sides)
    return join(
        live_blocks, block_aggregate, coarse, center, above, below, from_left, from_right
    )


def solution(mesh):
    placed = (
        P("stream", "cross", None, None),
        P("stream", "cross", None, None),
        P("stream", "cross", None),
        P("stream", "cross"),
        P("stream", "cross"),
        P("stream", "cross"),
    )
    return jax.shard_map(
        body,
        mesh=mesh,
        in_specs=placed,
        out_specs=P("stream", "cross", None, None),
        check_vma=False,
    )
```

```python
import jax
import jax.numpy as jnp
from jax import lax
from jax.experimental import pallas as pl
from jax.experimental.pallas import tpu as pltpu
from jax.sharding import PartitionSpec as P

BF16 = jnp.bfloat16
F32 = jnp.float32
MIB = 1 << 20
VMEM = pl.BlockSpec(memory_space=pltpu.VMEM)
SMEM = pl.BlockSpec(memory_space=pltpu.SMEM)


def swap_near(values, axis):
    count = lax.axis_size(axis)
    return lax.ppermute(values, axis, [(i, i ^ 1) for i in range(count) if i ^ 1 < count])


def swap_far(values, axis):
    count = lax.axis_size(axis)
    pairs = []
    for i in range(1, count - 1, 2):
        pairs += [(i, i + 1), (i + 1, i)]
    return lax.ppermute(values, axis, pairs)


def swap_bit(values, axis, bit):
    count = lax.axis_size(axis)
    return lax.ppermute(values, axis, [(i, i ^ bit) for i in range(count)])


def shaped(shape, dtype):
    return jax.ShapeDtypeStruct(shape, dtype)


def call(kernel, name, outs, ins, specs, out_specs, limit, flops=0, moved=0, scratch=()):
    return pl.pallas_call(
        kernel,
        out_shape=outs,
        in_specs=specs,
        out_specs=out_specs,
        scratch_shapes=list(scratch),
        cost_estimate=pl.CostEstimate(flops=flops, bytes_accessed=moved, transcendentals=0),
        compiler_params=pltpu.CompilerParams(vmem_limit_bytes=limit * MIB),
        name=name,
    )(*ins)


def parities(info_ref):
    return info_ref[1] % 2, info_ref[2] % 2


def mask_kernel(info_ref, residual_ref, near_ref, far_ref, cross_near, cross_far):
    rows, columns = residual_ref.shape[:2]
    half = rows // 2
    p, q = parities(info_ref)
    for out_ref, start in ((near_ref, half * (1 - p)), (far_ref, half * p)):
        for i in range(half):
            for j in range(columns):
                block = residual_ref[start + i, j]
                live = (start + i) * columns + j < info_ref[0]
                out_ref[i, j] = jnp.where(live, block, jnp.zeros_like(block))
    for out_ref, start in ((cross_near, (columns - 2) * (1 - q)), (cross_far, (columns - 2) * q)):
        for i in range(rows):
            for j in range(2):
                block = residual_ref[i, start + j]
                live = i * columns + start + j < info_ref[0]
                out_ref[i, j] = jnp.where(live, block, jnp.zeros_like(block))


def mask_blocks(info, residual):
    rows, columns, width, sides = residual.shape
    wide = shaped((rows // 2, columns, width, sides), BF16)
    tall = shaped((rows, 2, width, sides), BF16)
    return call(
        mask_kernel, "mask_blocks", (wide, wide, tall, tall), (info, residual),
        [SMEM, VMEM], (VMEM,) * 4, 4, moved=4 * residual.size,
    )


def payload_kernel(info_ref, agg_ref, near_ref, far_ref, inverse_ref, out_ref):
    unknowns, sides = near_ref.shape
    rows, columns = agg_ref.shape
    half = rows * columns * 2
    size = inverse_ref.shape[0]
    cells = unknowns // half
    p, _ = parities(info_ref)
    row = lax.broadcasted_iota(jnp.int32, (half, unknowns), 0)
    column = lax.broadcasted_iota(jnp.int32, (half, unknowns), 1)
    picks = jnp.where(column // cells == row, 1.0, 0.0).astype(BF16)
    for source, start in ((near_ref, half * (1 - p)), (far_ref, half * p)):
        sums = jnp.dot(picks, source[...], preferred_element_type=F32)
        out_ref[pl.ds(pl.multiple_of(start, half), half), :] = sums.astype(BF16)
    row = lax.broadcasted_iota(jnp.int32, (size, sides), 0)
    column = lax.broadcasted_iota(jnp.int32, (size, sides), 1)
    rest = inverse_ref[...]
    tail = jnp.zeros((size, sides), F32)
    for term in range(3):
        part = rest.astype(BF16)
        rest = rest - part.astype(F32)
        place = jnp.where(column == row + term * size, 1.0, 0.0).astype(BF16)
        tail = tail + jnp.dot(part, place, preferred_element_type=F32)
    lane = lax.broadcasted_iota(jnp.int32, (1, sides), 1) - 3 * size
    labels = jnp.zeros((1, sides), F32)
    for i in range(rows):
        for j in range(columns):
            labels = jnp.where(lane == i * columns + j, agg_ref[i, j].astype(F32), labels)
    out_ref[pl.ds(2 * half, size), :] = (tail + labels).astype(BF16)


def payload_of(info, agg, near, far, inverse):
    sides = near.shape[-1]
    rows, columns = agg.shape
    flat = (near.size // sides, sides)
    count = rows * columns * 4 + inverse.shape[0]
    return call(
        payload_kernel, "payload", shaped((1, count, sides), BF16),
        (info, agg, near.reshape(flat), far.reshape(flat), inverse),
        [SMEM, SMEM, VMEM, VMEM, VMEM], pl.BlockSpec((None, count, sides), lambda: (0, 0, 0)),
        6, flops=1 << 25, moved=4 * near.size,
    )


def join_pair_kernel(first_ref, second_ref, out_ref):
    count = first_ref.shape[0]
    out_ref[:count] = first_ref[...]
    out_ref[count:] = second_ref[...]


def join_pair(first, second):
    count = first.shape[0]
    return call(
        join_pair_kernel, "join_pair", shaped((2 * count,) + first.shape[1:], BF16),
        (first, second), [VMEM, VMEM], VMEM, 3, moved=8 * first.size,
    )


def corners_kernel(info_ref, cross_near, cross_far, near_ref, far_ref):
    half = near_ref.shape[0]
    p, _ = parities(info_ref)
    for out_ref, start in ((near_ref, half * (1 - p)), (far_ref, half * p)):
        for i in range(half):
            for j in range(2):
                out_ref[i, j] = cross_near[start + i, j]
                out_ref[i, 2 + j] = cross_far[start + i, j]


def corners(info, cross_near, cross_far):
    rows, _, width, sides = cross_near.shape
    piece = shaped((rows // 2, 4, width, sides), BF16)
    return call(
        corners_kernel, "corners", (piece, piece), (info, cross_near, cross_far),
        [SMEM, VMEM, VMEM], (VMEM, VMEM), 2, moved=8 * cross_near.size,
    )


def fix_of(pattern_ref, blocks_ref, grid_ref, n):
    picked = jnp.concatenate([grid_ref[pattern_ref[k, n]] for k in range(4)], axis=0)
    return jnp.dot(blocks_ref[n], picked, preferred_element_type=F32).astype(BF16)


def margin_kernel(
    info_ref, pattern_ref, blocks_ref,
    own_near, own_far, got_near, got_far, cross_near, cross_far, corner_near, corner_far,
    main_near, main_far, out_near, out_far, grid_ref,
):
    half, columns = own_near.shape[:2]
    rows = 2 * half
    wide = columns + 4
    p, q = parities(info_ref)
    near_row, far_row = (rows + 2) * (1 - p), (rows + 2) * p
    near_column, far_column = (columns + 2) * (1 - q), (columns + 2) * q
    for source, start in (
        (own_near, 2 + half * (1 - p)), (own_far, 2 + half * p),
        (got_near, near_row), (got_far, far_row),
    ):
        for i in range(2):
            for j in range(columns):
                grid_ref[(start + i) * wide + 2 + j] = source[i, j]
    for source, start in ((cross_near, near_column), (cross_far, far_column)):
        for i in range(rows):
            for j in range(2):
                grid_ref[(2 + i) * wide + start + j] = source[i, j]
    for source, start in ((corner_near, near_row), (corner_far, far_row)):
        for i in range(2):
            for j in range(2):
                grid_ref[(start + i) * wide + near_column + j] = source[i, j]
                grid_ref[(start + i) * wide + far_column + j] = source[i, 2 + j]
    for main, corner, start in ((main_near, out_near, near_row), (main_far, out_far, far_row)):
        for i in range(2):
            base = (start + i) * wide
            for j in range(2):
                corner[i, j] = fix_of(pattern_ref, blocks_ref, grid_ref, base + near_column + j)
                corner[i, 2 + j] = fix_of(pattern_ref, blocks_ref, grid_ref, base + far_column + j)
            for j in range(columns):
                main[i, j] = fix_of(pattern_ref, blocks_ref, grid_ref, base + 2 + j)


def margin_fixes(info, pattern, blocks, pieces):
    count, width, depth = blocks.shape
    half, columns, _, sides = pieces[0].shape
    main = shaped((2, columns, width, sides), BF16)
    corner = shaped((2, 4, width, sides), BF16)
    grid = shaped((count, width, sides), BF16)
    return call(
        margin_kernel, "margin_fixes", (main, main, corner, corner, grid),
        (info, pattern, blocks) + pieces, [SMEM, SMEM] + [VMEM] * 9, (VMEM,) * 5, 12,
        flops=blocks.size * sides, moved=2 * blocks.size,
    )


def center_kernel(info_ref, pattern_ref, blocks_ref, grid_ref, side_near, side_far, center_ref):
    rows, columns = center_ref.shape[:2]
    wide = columns + 4
    _, q = parities(info_ref)
    near_column, far_column = (columns + 2) * (1 - q), (columns + 2) * q
    for i in range(rows):
        base = (2 + i) * wide
        for j in range(2):
            side_near[i, j] = fix_of(pattern_ref, blocks_ref, grid_ref, base + near_column + j)
            side_far[i, j] = fix_of(pattern_ref, blocks_ref, grid_ref, base + far_column + j)
        for j in range(columns):
            center_ref[i, j] = fix_of(pattern_ref, blocks_ref, grid_ref, base + 2 + j)


def center_fixes(info, pattern, blocks, grid, rows, columns):
    _, width, sides = grid.shape
    side = shaped((rows, 2, width, sides), BF16)
    return call(
        center_kernel, "center_fixes",
        (side, side, shaped((rows, columns, width, sides), BF16)),
        (info, pattern, blocks, grid), [SMEM, SMEM, VMEM, VMEM], (VMEM,) * 3, 12,
        flops=blocks.size * sides, moved=2 * blocks.size,
    )


def fold_kernel(info_ref, side_near, side_far, corner_near, corner_far, out_near, out_far):
    half = corner_near.shape[0]
    p, _ = parities(info_ref)
    for source, start in ((corner_near, half * (1 - p)), (corner_far, half * p)):
        for i in range(half):
            for j in range(2):
                for side, out, at in ((side_near, out_near, j), (side_far, out_far, 2 + j)):
                    total = side[start + i, j].astype(F32) + source[i, at].astype(F32)
                    out[start + i, j] = total.astype(BF16)


def fold_sides(info, side_near, side_far, corner_near, corner_far):
    piece = shaped(side_near.shape, BF16)
    return call(
        fold_kernel, "fold_sides", (piece, piece),
        (info, side_near, side_far, corner_near, corner_far),
        [SMEM] + [VMEM] * 4, (VMEM, VMEM), 2, flops=2 * side_near.size, moved=12 * side_near.size,
    )


def split_dot(left, right):
    high = right.astype(BF16)
    low = (right - high.astype(F32)).astype(BF16)
    return jnp.dot(left, high, preferred_element_type=F32) + jnp.dot(
        left, low, preferred_element_type=F32
    )


def solve_kernel(bits, info_ref, agg_ref, first_ref, second_ref, out_ref, sums, coarse):
    count, height, sides = first_ref.shape
    rows, columns = agg_ref.shape
    fields = rows * columns * 4
    size = height - fields
    total = sums.shape[0]
    row = lax.broadcasted_iota(jnp.int32, (sides, fields), 0)
    column = lax.broadcasted_iota(jnp.int32, (sides, fields), 1)
    repeat = jnp.where(row - 3 * size == column // 4, 1.0, 0.0).astype(BF16)
    row = lax.broadcasted_iota(jnp.int32, (total, fields), 0)
    column = lax.broadcasted_iota(jnp.int32, (total, fields), 1)
    same_field = row % 4 == column % 4
    owner = (row // 4).astype(F32)
    for part, source in enumerate((first_ref, second_ref)):
        for k in range(count):
            tail = source[k, pl.ds(fields, 16), :]
            labels = jnp.dot(tail, repeat, preferred_element_type=F32)[:1]
            onehot = jnp.where(same_field & (owner == labels), 1.0, 0.0).astype(BF16)
            found = jnp.dot(
                onehot, source[k, pl.ds(0, fields), :], preferred_element_type=F32
            )
            if part == 0 and k == 0:
                sums[...] = found
            else:
                sums[...] += found
    for part, source in enumerate((first_ref, second_ref)):
        for k in range(count):
            slot, flips = part * count + k, 0
            for i, bit in enumerate(bits):
                if slot >> i & 1:
                    flips |= bit
            start = pl.multiple_of((info_ref[1] ^ flips) * size, size)
            mine = sums[pl.ds(start, size), :]
            stacked = jnp.concatenate([mine, mine, mine, jnp.zeros_like(mine)], axis=0)
            coarse[pl.ds(start, size), :] = split_dot(
                source[k, pl.ds(fields, size), :], stacked
            )
    row = lax.broadcasted_iota(jnp.int32, (fields, 1), 0)
    labels = jnp.zeros((fields, 1), jnp.int32)
    for i in range(rows):
        for j in range(columns):
            labels = jnp.where(row // 4 == i * columns + j, agg_ref[i, j], labels)
    row = lax.broadcasted_iota(jnp.int32, (fields, total), 0)
    column = lax.broadcasted_iota(jnp.int32, (fields, total), 1)
    onehot = jnp.where((column // 4 == labels) & (column % 4 == row % 4), 1.0, 0.0)
    out_ref[...] = split_dot(onehot.astype(BF16), coarse[...])


def coarse_values(bits, info, agg, first, second):
    count, height, sides = first.shape
    fields = agg.size * 4
    total = 2 * count * (height - fields)

    def kernel(*refs):
        solve_kernel(bits, *refs)

    return call(
        kernel, "coarse_values", shaped((fields, sides), F32), (info, agg, first, second),
        [SMEM, SMEM, VMEM, VMEM], VMEM, 8, flops=1 << 28, moved=4 * first.size,
        scratch=[pltpu.VMEM((total, sides), F32), pltpu.VMEM((total, sides), F32)],
    )


def join_kernel(
    info_ref, lifted_ref, center_ref, main_near, main_far, cross_near, cross_far, out_ref
):
    rows, columns, width, sides = center_ref.shape
    half = rows // 2
    cells = width // 4
    p, q = parities(info_ref)
    for i in range(rows):
        for j in range(columns):
            block = i * columns + j
            lifted = jnp.concatenate(
                [
                    jnp.broadcast_to(lifted_ref[pl.ds(block * 4 + f, 1), :], (cells, sides))
                    for f in range(4)
                ],
                axis=0,
            )
            out_ref[i, j] = center_ref[i, j].astype(F32) + lifted
    for source, start in ((main_near, half * (1 - p)), (main_far, half * p)):
        for i in range(half):
            for j in range(columns):
                out_ref[start + i, j] += source[i, j].astype(F32)
    for source, start in ((cross_near, (columns - 2) * (1 - q)), (cross_far, (columns - 2) * q)):
        for i in range(rows):
            for j in range(2):
                out_ref[i, start + j] += source[i, j].astype(F32)
    for i in range(rows):
        for j in range(columns):

            @pl.when(i * columns + j >= info_ref[0])
            def _(i=i, j=j):
                out_ref[i, j] = jnp.zeros((width, sides), F32)


def join(info, lifted, center, main_near, main_far, cross_near, cross_far):
    return call(
        join_kernel, "join", shaped(center.shape, F32),
        (info, lifted, center, main_near, main_far, cross_near, cross_far),
        [SMEM] + [VMEM] * 6, VMEM, 6, flops=8 * center.size, moved=10 * center.size,
    )


def body(residual, approx_inverse, pattern, live_blocks, block_aggregate, coarse_inverse):
    rows, columns = residual.shape[:2]
    info = jnp.stack([live_blocks[0, 0], lax.axis_index("stream"), lax.axis_index("cross")])
    own_near, own_far, edge_near, edge_far = mask_blocks(info, residual)
    bits = []
    while 2 << len(bits) <= lax.axis_size("stream"):
        bits.insert(0, 1 << len(bits))

    gathered = payload_of(info, block_aggregate, own_near, own_far, coarse_inverse)
    got_far = swap_far(own_far, "stream")
    got_near = swap_near(own_near, "stream")
    cross_far = swap_far(edge_far, "cross")
    cross_near = swap_near(edge_near, "cross")
    blocks, links = approx_inverse[0], jnp.transpose(pattern[0])
    got_far, got_near, cross_far, cross_near, blocks, gathered = lax.optimization_barrier(
        (got_far, got_near, cross_far, cross_near, blocks, gathered)
    )
    blocks = jnp.where(info[0] > 0, blocks, jnp.zeros((), BF16))
    corner_near, corner_far = corners(info, cross_near, cross_far)
    other = swap_bit(gathered, "stream", bits[0])
    corner_far = swap_far(corner_far, "stream")
    corner_near = swap_near(corner_near, "stream")
    gathered = join_pair(gathered, other)
    other = swap_bit(gathered, "stream", bits[1])
    gathered, corner_far, corner_near = lax.optimization_barrier(
        (gathered, corner_far, corner_near)
    )
    pieces = (own_near, own_far, got_near, got_far, cross_near, cross_far, corner_near, corner_far)
    main_near, main_far, corner_near, corner_far, grid = margin_fixes(info, links, blocks, pieces)
    corner_far, other = lax.optimization_barrier((corner_far, other))
    gathered = join_pair(gathered, other)
    corner_far = swap_far(corner_far, "stream")
    corner_near = swap_near(corner_near, "stream")
    other = swap_bit(gathered, "stream", bits[2])
    side_near, side_far, center = center_fixes(info, links, blocks, grid, rows, columns)
    side_near, other = lax.optimization_barrier((side_near, other))
    for bit in bits[3:]:
        gathered = join_pair(gathered, other)
        other = swap_bit(gathered, "stream", bit)
    gathered, corner_near, corner_far = lax.optimization_barrier(
        (gathered, corner_near, corner_far)
    )
    side_near, side_far = fold_sides(info, side_near, side_far, corner_near, corner_far)
    side_near, side_far, main_far, main_near = lax.optimization_barrier(
        (side_near, side_far, main_far, main_near)
    )
    main_far = swap_far(main_far, "stream")
    main_near = swap_near(main_near, "stream")
    cross_far = swap_far(side_far, "cross")
    cross_near = swap_near(side_near, "cross")
    lifted = coarse_values(bits, info, block_aggregate, gathered, other)
    return join(info, lifted, center, main_near, main_far, cross_near, cross_far)


def solution(mesh):
    placed = (
        P("stream", "cross", None, None),
        P("stream", "cross", None, None),
        P("stream", "cross", None),
        P("stream", "cross"),
        P("stream", "cross"),
        P("stream", "cross"),
    )
    return jax.shard_map(
        body,
        mesh=mesh,
        in_specs=placed,
        out_specs=P("stream", "cross", None, None),
        check_vma=False,
    )
```

```python
import jax
import jax.numpy as jnp
from jax import lax
from jax.experimental import pallas as pl
from jax.experimental.pallas import tpu as pltpu
from jax.sharding import PartitionSpec as P

BF16 = jnp.bfloat16
F32 = jnp.float32
MIB = 1 << 20
VMEM = pl.BlockSpec(memory_space=pltpu.VMEM)
SMEM = pl.BlockSpec(memory_space=pltpu.SMEM)


def swap_near(values, axis):
    count = lax.axis_size(axis)
    return lax.ppermute(values, axis, [(i, i ^ 1) for i in range(count) if i ^ 1 < count])


def swap_far(values, axis):
    count = lax.axis_size(axis)
    pairs = []
    for i in range(1, count - 1, 2):
        pairs += [(i, i + 1), (i + 1, i)]
    return lax.ppermute(values, axis, pairs)


def swap_halves(values, axis):
    count = lax.axis_size(axis)
    return lax.ppermute(values, axis, [(i, (i + count // 2) % count) for i in range(count)])


def exchange_in_half(values, axis):
    half = lax.axis_size(axis) // 2
    groups = [list(range(half)), list(range(half, 2 * half))]
    return lax.all_to_all(values, axis, 0, 0, axis_index_groups=groups)


def shaped(shape, dtype):
    return jax.ShapeDtypeStruct(shape, dtype)


def call(kernel, name, outs, ins, specs, out_specs, limit, flops=0, moved=0, scratch=()):
    return pl.pallas_call(
        kernel,
        out_shape=outs,
        in_specs=specs,
        out_specs=out_specs,
        scratch_shapes=list(scratch),
        cost_estimate=pl.CostEstimate(flops=flops, bytes_accessed=moved, transcendentals=0),
        compiler_params=pltpu.CompilerParams(vmem_limit_bytes=limit * MIB),
        name=name,
    )(*ins)


def parities(info_ref):
    return info_ref[1] % 2, info_ref[2] % 2


def mask_kernel(info_ref, residual_ref, near_ref, far_ref, cross_near, cross_far):
    rows, columns = residual_ref.shape[:2]
    half = rows // 2
    p, q = parities(info_ref)
    for out_ref, start in ((near_ref, half * (1 - p)), (far_ref, half * p)):
        for i in range(half):
            for j in range(columns):
                block = residual_ref[start + i, j]
                live = (start + i) * columns + j < info_ref[0]
                out_ref[i, j] = jnp.where(live, block, jnp.zeros_like(block))
    for out_ref, start in ((cross_near, (columns - 2) * (1 - q)), (cross_far, (columns - 2) * q)):
        for i in range(rows):
            for j in range(2):
                block = residual_ref[i, start + j]
                live = i * columns + start + j < info_ref[0]
                out_ref[i, j] = jnp.where(live, block, jnp.zeros_like(block))


def mask_blocks(info, residual):
    rows, columns, width, sides = residual.shape
    wide = shaped((rows // 2, columns, width, sides), BF16)
    tall = shaped((rows, 2, width, sides), BF16)
    return call(
        mask_kernel, "mask_blocks", (wide, wide, tall, tall), (info, residual),
        [SMEM, VMEM], (VMEM,) * 4, 4, moved=4 * residual.size,
    )


def payload_kernel(info_ref, agg_ref, near_ref, far_ref, inverse_ref, out_ref):
    unknowns, sides = near_ref.shape
    rows, columns = agg_ref.shape
    half = rows * columns * 2
    size = inverse_ref.shape[0]
    cells = unknowns // half
    p, _ = parities(info_ref)
    row = lax.broadcasted_iota(jnp.int32, (half, unknowns), 0)
    column = lax.broadcasted_iota(jnp.int32, (half, unknowns), 1)
    picks = jnp.where(column // cells == row, 1.0, 0.0).astype(BF16)
    for source, start in ((near_ref, half * (1 - p)), (far_ref, half * p)):
        sums = jnp.dot(picks, source[...], preferred_element_type=F32)
        out_ref[pl.ds(pl.multiple_of(start, half), half), :] = sums.astype(BF16)
    row = lax.broadcasted_iota(jnp.int32, (size, sides), 0)
    column = lax.broadcasted_iota(jnp.int32, (size, sides), 1)
    rest = inverse_ref[...]
    tail = jnp.zeros((size, sides), F32)
    for term in range(3):
        part = rest.astype(BF16)
        rest = rest - part.astype(F32)
        place = jnp.where(column == row + term * size, 1.0, 0.0).astype(BF16)
        tail = tail + jnp.dot(part, place, preferred_element_type=F32)
    lane = lax.broadcasted_iota(jnp.int32, (1, sides), 1) - 3 * size
    labels = jnp.zeros((1, sides), F32)
    for i in range(rows):
        for j in range(columns):
            labels = jnp.where(lane == i * columns + j, agg_ref[i, j].astype(F32), labels)
    out_ref[pl.ds(2 * half, size), :] = (tail + labels).astype(BF16)


def payload_of(info, agg, near, far, inverse):
    sides = near.shape[-1]
    rows, columns = agg.shape
    flat = (near.size // sides, sides)
    count = rows * columns * 4 + inverse.shape[0]
    return call(
        payload_kernel, "payload", shaped((1, count, sides), BF16),
        (info, agg, near.reshape(flat), far.reshape(flat), inverse),
        [SMEM, SMEM, VMEM, VMEM, VMEM], pl.BlockSpec((None, count, sides), lambda: (0, 0, 0)),
        6, flops=1 << 25, moved=4 * near.size,
    )


def spread_kernel(first_ref, second_ref, out_ref):
    for i in range(out_ref.shape[0]):
        out_ref[i, 0] = first_ref[0]
        out_ref[i, 1] = second_ref[0]


def spread_pair(first, second, copies):
    return call(
        spread_kernel, "spread_pair", shaped((copies, 2) + first.shape[1:], BF16),
        (first, second), [VMEM, VMEM], VMEM, 3, moved=4 * copies * first.size,
    )


def corners_kernel(info_ref, own_near, cross_near, cross_far, near_ref, far_ref):
    half, columns = own_near.shape[:2]
    p, _ = parities(info_ref)
    for i in range(half):
        for j in range(columns):
            near_ref[i, j] = own_near[i, j]
    for out_ref, start, base in ((near_ref, half * (1 - p), columns), (far_ref, half * p, 0)):
        for i in range(half):
            for j in range(2):
                out_ref[i, base + j] = cross_near[start + i, j]
                out_ref[i, base + 2 + j] = cross_far[start + i, j]


def corners(info, own_near, cross_near, cross_far):
    half, columns, width, sides = own_near.shape
    return call(
        corners_kernel, "corners",
        (shaped((half, columns + 4, width, sides), BF16), shaped((half, 4, width, sides), BF16)),
        (info, own_near, cross_near, cross_far), [SMEM, VMEM, VMEM, VMEM], (VMEM, VMEM), 3,
        moved=8 * cross_near.size,
    )


def fix_of(pattern_ref, blocks_ref, grid_ref, n):
    picked = jnp.concatenate([grid_ref[pattern_ref[k, n]] for k in range(4)], axis=0)
    return jnp.dot(blocks_ref[n], picked, preferred_element_type=F32).astype(BF16)


def margin_kernel(
    info_ref, pattern_ref, blocks_ref,
    own_near, own_far, got_near, got_far, cross_near, cross_far, corner_far,
    out_near, main_far, out_far, grid_ref,
):
    half, columns = own_near.shape[:2]
    rows = 2 * half
    wide = columns + 4
    p, q = parities(info_ref)
    near_row, far_row = (rows + 2) * (1 - p), (rows + 2) * p
    near_column, far_column = (columns + 2) * (1 - q), (columns + 2) * q
    for source, start in (
        (own_near, 2 + half * (1 - p)), (own_far, 2 + half * p),
        (got_near, near_row), (got_far, far_row),
    ):
        for i in range(2):
            for j in range(columns):
                grid_ref[(start + i) * wide + 2 + j] = source[i, j]
    for source, start in ((cross_near, near_column), (cross_far, far_column)):
        for i in range(rows):
            for j in range(2):
                grid_ref[(2 + i) * wide + start + j] = source[i, j]
    for source, start, first in ((got_near, near_row, columns), (corner_far, far_row, 0)):
        for i in range(2):
            for j in range(2):
                grid_ref[(start + i) * wide + near_column + j] = source[i, first + j]
                grid_ref[(start + i) * wide + far_column + j] = source[i, first + 2 + j]
    for main, corner, first, start in (
        (main_far, out_far, 0, far_row), (out_near, out_near, columns, near_row)
    ):
        for i in range(2):
            base = (start + i) * wide
            for j in range(2):
                corner[i, first + j] = fix_of(
                    pattern_ref, blocks_ref, grid_ref, base + near_column + j
                )
                corner[i, first + 2 + j] = fix_of(
                    pattern_ref, blocks_ref, grid_ref, base + far_column + j
                )
            for j in range(columns):
                main[i, j] = fix_of(pattern_ref, blocks_ref, grid_ref, base + 2 + j)


def margin_fixes(info, pattern, blocks, pieces):
    count, width, depth = blocks.shape
    half, columns, _, sides = pieces[0].shape
    near = shaped((2, columns + 4, width, sides), BF16)
    main = shaped((2, columns, width, sides), BF16)
    corner = shaped((2, 4, width, sides), BF16)
    grid = shaped((count, width, sides), BF16)
    return call(
        margin_kernel, "margin_fixes", (near, main, corner, grid),
        (info, pattern, blocks) + pieces, [SMEM, SMEM] + [VMEM] * 8, (VMEM,) * 4, 12,
        flops=blocks.size * sides, moved=2 * blocks.size,
    )


def center_kernel(info_ref, pattern_ref, blocks_ref, grid_ref, side_near, side_far, center_ref):
    rows, columns = center_ref.shape[:2]
    wide = columns + 4
    _, q = parities(info_ref)
    near_column, far_column = (columns + 2) * (1 - q), (columns + 2) * q
    for i in range(rows):
        base = (2 + i) * wide
        for j in range(2):
            side_near[i, j] = fix_of(pattern_ref, blocks_ref, grid_ref, base + near_column + j)
            side_far[i, j] = fix_of(pattern_ref, blocks_ref, grid_ref, base + far_column + j)
        for j in range(columns):
            center_ref[i, j] = fix_of(pattern_ref, blocks_ref, grid_ref, base + 2 + j)


def center_fixes(info, pattern, blocks, grid, rows, columns):
    _, width, sides = grid.shape
    side = shaped((rows, 2, width, sides), BF16)
    return call(
        center_kernel, "center_fixes",
        (side, side, shaped((rows, columns, width, sides), BF16)),
        (info, pattern, blocks, grid), [SMEM, SMEM, VMEM, VMEM], (VMEM,) * 3, 12,
        flops=blocks.size * sides, moved=2 * blocks.size,
    )


def fold_kernel(info_ref, side_near, side_far, got_near, corner_far, out_near, out_far):
    half, wide = got_near.shape[:2]
    p, _ = parities(info_ref)
    for source, start, first in (
        (got_near, half * (1 - p), wide - 4), (corner_far, half * p, 0)
    ):
        for i in range(half):
            for j in range(2):
                for side, out, at in ((side_near, out_near, j), (side_far, out_far, 2 + j)):
                    total = side[start + i, j].astype(F32) + source[i, first + at].astype(F32)
                    out[start + i, j] = total.astype(BF16)


def fold_sides(info, side_near, side_far, got_near, corner_far):
    piece = shaped(side_near.shape, BF16)
    return call(
        fold_kernel, "fold_sides", (piece, piece),
        (info, side_near, side_far, got_near, corner_far),
        [SMEM] + [VMEM] * 4, (VMEM, VMEM), 3, flops=2 * side_near.size, moved=12 * side_near.size,
    )


def split_dot(left, right):
    high = right.astype(BF16)
    low = (right - high.astype(F32)).astype(BF16)
    return jnp.dot(left, high, preferred_element_type=F32) + jnp.dot(
        left, low, preferred_element_type=F32
    )


def solve_kernel(info_ref, agg_ref, gathered_ref, out_ref, sums, coarse):
    count, pair, height, sides = gathered_ref.shape
    rows, columns = agg_ref.shape
    fields = rows * columns * 4
    size = height - fields
    total = sums.shape[0]
    row = lax.broadcasted_iota(jnp.int32, (sides, fields), 0)
    column = lax.broadcasted_iota(jnp.int32, (sides, fields), 1)
    repeat = jnp.where(row - 3 * size == column // 4, 1.0, 0.0).astype(BF16)
    row = lax.broadcasted_iota(jnp.int32, (total, fields), 0)
    column = lax.broadcasted_iota(jnp.int32, (total, fields), 1)
    same_field = row % 4 == column % 4
    owner = (row // 4).astype(F32)
    slots = [(k, i) for k in range(count) for i in range(pair)]
    for place, (k, i) in enumerate(slots):
        tail = gathered_ref[k, i, pl.ds(fields, 16), :]
        labels = jnp.dot(tail, repeat, preferred_element_type=F32)[:1]
        onehot = jnp.where(same_field & (owner == labels), 1.0, 0.0).astype(BF16)
        found = jnp.dot(
            onehot, gathered_ref[k, i, pl.ds(0, fields), :], preferred_element_type=F32
        )
        if place == 0:
            sums[...] = found
        else:
            sums[...] += found
    high = info_ref[1] // count
    for k, i in slots:
        start = pl.multiple_of((k + count * (high ^ i)) * size, size)
        mine = sums[pl.ds(start, size), :]
        stacked = jnp.concatenate([mine, mine, mine, jnp.zeros_like(mine)], axis=0)
        coarse[pl.ds(start, size), :] = split_dot(
            gathered_ref[k, i, pl.ds(fields, size), :], stacked
        )
    row = lax.broadcasted_iota(jnp.int32, (fields, 1), 0)
    labels = jnp.zeros((fields, 1), jnp.int32)
    for i in range(rows):
        for j in range(columns):
            labels = jnp.where(row // 4 == i * columns + j, agg_ref[i, j], labels)
    row = lax.broadcasted_iota(jnp.int32, (fields, total), 0)
    column = lax.broadcasted_iota(jnp.int32, (fields, total), 1)
    onehot = jnp.where((column // 4 == labels) & (column % 4 == row % 4), 1.0, 0.0)
    out_ref[...] = split_dot(onehot.astype(BF16), coarse[...])


def coarse_values(info, agg, gathered):
    count, pair, height, sides = gathered.shape
    fields = agg.size * 4
    total = count * pair * (height - fields)
    return call(
        solve_kernel, "coarse_values", shaped((fields, sides), F32), (info, agg, gathered),
        [SMEM, SMEM, VMEM], VMEM, 8, flops=1 << 28, moved=2 * gathered.size,
        scratch=[pltpu.VMEM((total, sides), F32), pltpu.VMEM((total, sides), F32)],
    )


def join_kernel(
    info_ref, lifted_ref, center_ref, main_near, main_far, cross_near, cross_far, out_ref
):
    rows, columns, width, sides = center_ref.shape
    half = rows // 2
    cells = width // 4
    p, q = parities(info_ref)
    for i in range(rows):
        for j in range(columns):
            block = i * columns + j
            lifted = jnp.concatenate(
                [
                    jnp.broadcast_to(lifted_ref[pl.ds(block * 4 + f, 1), :], (cells, sides))
                    for f in range(4)
                ],
                axis=0,
            )
            out_ref[i, j] = center_ref[i, j].astype(F32) + lifted
    for source, start in ((main_near, half * (1 - p)), (main_far, half * p)):
        for i in range(half):
            for j in range(columns):
                out_ref[start + i, j] += source[i, j].astype(F32)
    for source, start in ((cross_near, (columns - 2) * (1 - q)), (cross_far, (columns - 2) * q)):
        for i in range(rows):
            for j in range(2):
                out_ref[i, start + j] += source[i, j].astype(F32)
    for i in range(rows):
        for j in range(columns):

            @pl.when(i * columns + j >= info_ref[0])
            def _(i=i, j=j):
                out_ref[i, j] = jnp.zeros((width, sides), F32)


def join(info, lifted, center, main_near, main_far, cross_near, cross_far):
    return call(
        join_kernel, "join", shaped(center.shape, F32),
        (info, lifted, center, main_near, main_far, cross_near, cross_far),
        [SMEM] + [VMEM] * 6, VMEM, 6, flops=8 * center.size, moved=10 * center.size,
    )


def body(residual, approx_inverse, pattern, live_blocks, block_aggregate, coarse_inverse):
    rows, columns = residual.shape[:2]
    info = jnp.stack([live_blocks[0, 0], lax.axis_index("stream"), lax.axis_index("cross")])
    own_near, own_far, edge_near, edge_far = mask_blocks(info, residual)
    gathered = payload_of(info, block_aggregate, own_near, own_far, coarse_inverse)
    got_far = swap_far(own_far, "stream")
    cross_far = swap_far(edge_far, "cross")
    cross_near = swap_near(edge_near, "cross")
    blocks, links = approx_inverse[0], jnp.transpose(pattern[0])
    blocks, gathered = lax.optimization_barrier((blocks, gathered))
    blocks = jnp.where(info[0] > 0, blocks, jnp.zeros((), BF16))
    other = swap_halves(gathered, "stream")
    got_far, cross_far, cross_near, blocks = lax.optimization_barrier(
        (got_far, cross_far, cross_near, blocks)
    )
    got_near, corner_far = corners(info, own_near, cross_near, cross_far)
    corner_far = swap_far(corner_far, "stream")
    got_near = swap_near(got_near, "stream")
    gathered = spread_pair(gathered, other, lax.axis_size("stream") // 2)
    gathered = exchange_in_half(gathered, "stream")
    pieces = (own_near, own_far, got_near, got_far, cross_near, cross_far, corner_far)
    near, main_far, corner_far, grid = margin_fixes(info, links, blocks, pieces)
    corner_far = swap_far(corner_far, "stream")
    near = swap_near(near, "stream")
    side_near, side_far, center = center_fixes(info, links, blocks, grid, rows, columns)
    side_near, side_far = fold_sides(info, side_near, side_far, near, corner_far)
    main_far = swap_far(main_far, "stream")
    cross_far = swap_far(side_far, "cross")
    cross_near = swap_near(side_near, "cross")
    lifted = coarse_values(info, block_aggregate, gathered)
    return join(info, lifted, center, near, main_far, cross_near, cross_far)


def solution(mesh):
    placed = (
        P("stream", "cross", None, None),
        P("stream", "cross", None, None),
        P("stream", "cross", None),
        P("stream", "cross"),
        P("stream", "cross"),
        P("stream", "cross"),
    )
    return jax.shard_map(
        body,
        mesh=mesh,
        in_specs=placed,
        out_specs=P("stream", "cross", None, None),
        check_vma=False,
    )
```

```python
import jax
import jax.numpy as jnp
from jax import lax
from jax.experimental import pallas as pl
from jax.experimental.pallas import tpu as pltpu
from jax.sharding import PartitionSpec as P

BF16 = jnp.bfloat16
F32 = jnp.float32
MIB = 1 << 20
VMEM = pl.BlockSpec(memory_space=pltpu.VMEM)
SMEM = pl.BlockSpec(memory_space=pltpu.SMEM)


def swap_near(values, axis):
    count = lax.axis_size(axis)
    return lax.ppermute(values, axis, [(i, i ^ 1) for i in range(count) if i ^ 1 < count])


def swap_far(values, axis):
    count = lax.axis_size(axis)
    pairs = []
    for i in range(1, count - 1, 2):
        pairs += [(i, i + 1), (i + 1, i)]
    return lax.ppermute(values, axis, pairs)


def far_of(index):
    return index + 1 if index % 2 else index - 1


def swap_diagonal(values, other):
    count, wide = lax.axis_size("stream"), lax.axis_size("cross")
    pairs = []
    for i in range(count):
        for j in range(wide):
            k, m = far_of(i), other(j)
            if 0 <= k < count and 0 <= m < wide:
                pairs.append((i * wide + j, k * wide + m))
    return lax.ppermute(values, ("stream", "cross"), pairs)


def swap_halves(values, axis):
    count = lax.axis_size(axis)
    return lax.ppermute(values, axis, [(i, (i + count // 2) % count) for i in range(count)])


def exchange_in_half(values, axis):
    half = lax.axis_size(axis) // 2
    groups = [list(range(half)), list(range(half, 2 * half))]
    return lax.all_to_all(values, axis, 0, 0, axis_index_groups=groups)


def shaped(shape, dtype):
    return jax.ShapeDtypeStruct(shape, dtype)


def call(kernel, name, outs, ins, specs, out_specs, limit, flops=0, moved=0, scratch=()):
    return pl.pallas_call(
        kernel,
        out_shape=outs,
        in_specs=specs,
        out_specs=out_specs,
        scratch_shapes=list(scratch),
        cost_estimate=pl.CostEstimate(flops=flops, bytes_accessed=moved, transcendentals=0),
        compiler_params=pltpu.CompilerParams(vmem_limit_bytes=limit * MIB),
        name=name,
    )(*ins)


def parities(info_ref):
    return info_ref[1] % 2, info_ref[2] % 2


def mask_kernel(
    info_ref, residual_ref, near_ref, far_ref, cross_near, cross_far, corner_near, corner_far
):
    rows, columns = residual_ref.shape[:2]
    half = rows // 2
    p, q = parities(info_ref)
    for out_ref, start in ((near_ref, half * (1 - p)), (far_ref, half * p)):
        for i in range(half):
            for j in range(columns):
                block = residual_ref[start + i, j]
                live = (start + i) * columns + j < info_ref[0]
                out_ref[i, j] = jnp.where(live, block, jnp.zeros_like(block))
    for out_ref, corner, start in (
        (cross_near, corner_near, (columns - 2) * (1 - q)),
        (cross_far, corner_far, (columns - 2) * q),
    ):
        for i in range(rows):
            for j in range(2):
                block = residual_ref[i, start + j]
                live = i * columns + start + j < info_ref[0]
                out_ref[i, j] = jnp.where(live, block, jnp.zeros_like(block))
        for i in range(half):
            for j in range(2):
                corner[i, j] = far_ref[i, start + j]


def mask_blocks(info, residual):
    rows, columns, width, sides = residual.shape
    wide = shaped((rows // 2, columns, width, sides), BF16)
    tall = shaped((rows, 2, width, sides), BF16)
    corner = shaped((rows // 2, 2, width, sides), BF16)
    return call(
        mask_kernel, "mask_blocks", (wide, wide, tall, tall, corner, corner), (info, residual),
        [SMEM, VMEM], (VMEM,) * 6, 4, moved=4 * residual.size,
    )


def split_dot(left, right):
    high = right.astype(BF16)
    low = (right - high.astype(F32)).astype(BF16)
    return jnp.dot(left, high, preferred_element_type=F32) + jnp.dot(
        left, low, preferred_element_type=F32
    )


def aggregate_at(index, half, size):
    per = size // 4
    slot, rest = index // (2 * size), index % (2 * size)
    return (slot + half * (rest // size)) * per + rest % size // 4


def partial_kernel(info_ref, agg_ref, near_ref, far_ref, out_ref, sums_ref):
    unknowns, sides = near_ref.shape
    rows, columns = agg_ref.shape
    fields = rows * columns * 2
    cells = unknowns // fields
    slots, height, _ = out_ref.shape
    p, _ = parities(info_ref)
    row = lax.broadcasted_iota(jnp.int32, (fields, unknowns), 0)
    column = lax.broadcasted_iota(jnp.int32, (fields, unknowns), 1)
    picks = jnp.where(column // cells == row, 1.0, 0.0).astype(BF16)
    for source, start in ((near_ref, fields * (1 - p)), (far_ref, fields * p)):
        sums_ref[pl.ds(pl.multiple_of(start, fields), fields), :] = jnp.dot(
            picks, source[...], preferred_element_type=F32
        )
    lane = lax.broadcasted_iota(jnp.int32, (1, 2 * fields), 1) // 4
    labels = jnp.zeros((1, 2 * fields), jnp.int32)
    for i in range(rows):
        for j in range(columns):
            labels = jnp.where(lane == i * columns + j, agg_ref[i, j], labels)
    shape = (slots * height, 2 * fields)
    row = lax.broadcasted_iota(jnp.int32, (shape[0], 1), 0)
    label = aggregate_at(row, slots, height // 2)
    column = lax.broadcasted_iota(jnp.int32, shape, 1)
    row = lax.broadcasted_iota(jnp.int32, shape, 0)
    onehot = jnp.where((label == labels) & (row % 4 == column % 4), 1.0, 0.0)
    found = split_dot(onehot.astype(BF16), sums_ref[...])
    out_ref[...] = found.astype(BF16).reshape(out_ref.shape)


def partial_sums(info, agg, near, far, slots, size):
    sides = near.shape[-1]
    flat = (near.size // sides, sides)
    return call(
        partial_kernel, "partial_sums", shaped((slots, 2 * size, sides), BF16),
        (info, agg, near.reshape(flat), far.reshape(flat)), [SMEM, SMEM, VMEM, VMEM], VMEM, 6,
        flops=1 << 25, moved=4 * near.size,
        scratch=[pltpu.VMEM((agg.size * 4, sides), F32)],
    )


def half_kernel(parts_ref, inverse_ref, out_ref):
    slots, height, sides = parts_ref.shape
    size = inverse_ref.shape[0]
    total = parts_ref[0].astype(F32)
    for i in range(1, slots):
        total = total + parts_ref[i].astype(F32)
    out_ref[:height] = total.astype(BF16)
    row = lax.broadcasted_iota(jnp.int32, (size, sides), 0)
    column = lax.broadcasted_iota(jnp.int32, (size, sides), 1)
    rest = inverse_ref[...]
    tail = jnp.zeros((size, sides), F32)
    for term in range(3):
        part = rest.astype(BF16)
        rest = rest - part.astype(F32)
        place = jnp.where(column == row + term * size, 1.0, 0.0).astype(BF16)
        tail = tail + jnp.dot(part, place, preferred_element_type=F32)
    out_ref[height:] = tail.astype(BF16)


def half_sums(parts, inverse):
    _, height, sides = parts.shape
    size = inverse.shape[0]
    return call(
        half_kernel, "half_sums", shaped((height + size, sides), BF16), (parts, inverse),
        [VMEM, VMEM], VMEM, 2, flops=4 * parts.size, moved=2 * parts.size,
    )


def solve_kernel(info_ref, own_ref, other_ref, out_ref):
    slots, height, sides = out_ref.shape
    size = height // 2
    high = info_ref[1] // slots
    for source, u in ((own_ref, high), (other_ref, 1 - high)):
        start = pl.multiple_of(u * size, size)
        mine = own_ref[pl.ds(start, size), :].astype(F32)
        mine = mine + other_ref[pl.ds(start, size), :].astype(F32)
        stacked = jnp.concatenate([mine, mine, mine, jnp.zeros_like(mine)], axis=0)
        coarse = split_dot(source[pl.ds(height, size), :], stacked).astype(BF16)
        for i in range(slots):
            out_ref[i, pl.ds(start, size), :] = coarse


def coarse_solve(info, own, other, slots, size):
    sides = own.shape[-1]
    return call(
        solve_kernel, "coarse_solve", shaped((slots, 2 * size, sides), BF16),
        (info, own, other), [SMEM, VMEM, VMEM], VMEM, 2, flops=1 << 22, moved=4 * own.size,
    )


def near_kernel(info_ref, own_near, cross_near, cross_far, near_ref):
    half, columns = own_near.shape[:2]
    p, _ = parities(info_ref)
    start = half * (1 - p)
    for i in range(half):
        for j in range(columns):
            near_ref[i, j] = own_near[i, j]
        for j in range(2):
            near_ref[i, columns + j] = cross_near[start + i, j]
            near_ref[i, columns + 2 + j] = cross_far[start + i, j]


def near_message(info, own_near, cross_near, cross_far):
    half, columns, width, sides = own_near.shape
    return call(
        near_kernel, "near_message", shaped((half, columns + 4, width, sides), BF16),
        (info, own_near, cross_near, cross_far), [SMEM, VMEM, VMEM, VMEM], VMEM, 3,
        moved=8 * cross_near.size,
    )


def fix_of(pattern_ref, blocks_ref, grid_ref, n):
    picked = jnp.concatenate([grid_ref[pattern_ref[k, n]] for k in range(4)], axis=0)
    return jnp.dot(blocks_ref[n], picked, preferred_element_type=F32).astype(BF16)


def margin_kernel(
    info_ref, pattern_ref, blocks_ref,
    own_near, own_far, got_near, got_far, cross_near, cross_far, got_corner_near, got_corner_far,
    out_near, out_far, corner_near, corner_far, grid_ref,
):
    half, columns = own_near.shape[:2]
    rows = 2 * half
    wide = columns + 4
    p, q = parities(info_ref)
    near_row, far_row = (rows + 2) * (1 - p), (rows + 2) * p
    near_column, far_column = (columns + 2) * (1 - q), (columns + 2) * q
    for source, start in (
        (own_near, 2 + half * (1 - p)), (own_far, 2 + half * p),
        (got_near, near_row), (got_far, far_row),
    ):
        for i in range(2):
            for j in range(columns):
                grid_ref[(start + i) * wide + 2 + j] = source[i, j]
    for source, start in ((cross_near, near_column), (cross_far, far_column)):
        for i in range(rows):
            for j in range(2):
                grid_ref[(2 + i) * wide + start + j] = source[i, j]
    for i in range(2):
        for j in range(2):
            near, far = (near_row + i) * wide + j, (far_row + i) * wide + j
            grid_ref[near + near_column] = got_near[i, columns + j]
            grid_ref[near + far_column] = got_near[i, columns + 2 + j]
            grid_ref[far + near_column] = got_corner_near[i, j]
            grid_ref[far + far_column] = got_corner_far[i, j]

    def fix(n):
        return fix_of(pattern_ref, blocks_ref, grid_ref, n)

    for i in range(2):
        near, far = (near_row + i) * wide, (far_row + i) * wide
        for j in range(columns):
            out_far[i, j] = fix(far + 2 + j)
            out_near[i, j] = fix(near + 2 + j)
        for j in range(2):
            corner_near[i, j] = fix(far + near_column + j)
            corner_far[i, j] = fix(far + far_column + j)
            out_near[i, columns + j] = fix(near + near_column + j)
            out_near[i, columns + 2 + j] = fix(near + far_column + j)


def margin_fixes(info, pattern, blocks, pieces):
    count, width, depth = blocks.shape
    half, columns, _, sides = pieces[0].shape
    near = shaped((2, columns + 4, width, sides), BF16)
    main = shaped((2, columns, width, sides), BF16)
    corner = shaped((2, 2, width, sides), BF16)
    grid = shaped((count, width, sides), BF16)
    return call(
        margin_kernel, "margin_fixes", (near, main, corner, corner, grid),
        (info, pattern, blocks) + pieces, [SMEM, SMEM] + [VMEM] * 9, (VMEM,) * 5, 12,
        flops=blocks.size * sides, moved=2 * blocks.size,
    )


def center_kernel(info_ref, pattern_ref, blocks_ref, grid_ref, side_near, side_far, center_ref):
    rows, columns = center_ref.shape[:2]
    wide = columns + 4
    _, q = parities(info_ref)
    near_column, far_column = (columns + 2) * (1 - q), (columns + 2) * q
    for i in range(rows):
        base = (2 + i) * wide
        for j in range(2):
            side_near[i, j] = fix_of(pattern_ref, blocks_ref, grid_ref, base + near_column + j)
            side_far[i, j] = fix_of(pattern_ref, blocks_ref, grid_ref, base + far_column + j)
        for j in range(columns):
            center_ref[i, j] = fix_of(pattern_ref, blocks_ref, grid_ref, base + 2 + j)


def center_fixes(info, pattern, blocks, grid, rows, columns):
    _, width, sides = grid.shape
    side = shaped((rows, 2, width, sides), BF16)
    return call(
        center_kernel, "center_fixes",
        (side, side, shaped((rows, columns, width, sides), BF16)),
        (info, pattern, blocks, grid), [SMEM, SMEM, VMEM, VMEM], (VMEM,) * 3, 12,
        flops=blocks.size * sides, moved=2 * blocks.size,
    )


def fold_kernel(info_ref, side_near, side_far, got_near, out_near, out_far):
    half, wide = got_near.shape[:2]
    p, _ = parities(info_ref)
    fold, keep = half * (1 - p), half * p
    for i in range(half):
        for j in range(2):
            for side, out, at in ((side_near, out_near, j), (side_far, out_far, 2 + j)):
                total = side[fold + i, j].astype(F32) + got_near[i, wide - 4 + at].astype(F32)
                out[fold + i, j] = total.astype(BF16)
                out[keep + i, j] = side[keep + i, j]


def fold_sides(info, side_near, side_far, got_near):
    piece = shaped(side_near.shape, BF16)
    return call(
        fold_kernel, "fold_sides", (piece, piece), (info, side_near, side_far, got_near),
        [SMEM] + [VMEM] * 3, (VMEM, VMEM), 3, flops=2 * side_near.size, moved=12 * side_near.size,
    )


def lift_kernel(agg_ref, coarse_ref, out_ref):
    slots, height, sides = coarse_ref.shape
    rows, columns = agg_ref.shape
    fields = rows * columns * 4
    shape = (fields, slots * height)
    row = lax.broadcasted_iota(jnp.int32, (fields, 1), 0) // 4
    labels = jnp.zeros((fields, 1), jnp.int32)
    for i in range(rows):
        for j in range(columns):
            labels = jnp.where(row == i * columns + j, agg_ref[i, j], labels)
    column = lax.broadcasted_iota(jnp.int32, (1, shape[1]), 1)
    label = aggregate_at(column, slots, height // 2)
    row = lax.broadcasted_iota(jnp.int32, shape, 0)
    column = lax.broadcasted_iota(jnp.int32, shape, 1)
    onehot = jnp.where((label == labels) & (column % 4 == row % 4), 1.0, 0.0)
    coarse = coarse_ref[...].reshape(shape[1], sides)
    out_ref[...] = jnp.dot(onehot.astype(BF16), coarse, preferred_element_type=F32)


def lift(agg, coarse):
    sides = coarse.shape[-1]
    return call(
        lift_kernel, "lift", shaped((agg.size * 4, sides), F32), (agg, coarse), [SMEM, VMEM],
        VMEM, 3, flops=1 << 24, moved=2 * coarse.size,
    )


def join_kernel(
    info_ref, lifted_ref, center_ref, main_near, main_far, cross_near, cross_far,
    corner_near, corner_far, out_ref,
):
    rows, columns, width, sides = center_ref.shape
    half = rows // 2
    cells = width // 4
    p, q = parities(info_ref)
    for i in range(rows):
        for j in range(columns):
            block = i * columns + j
            lifted = jnp.concatenate(
                [
                    jnp.broadcast_to(lifted_ref[pl.ds(block * 4 + f, 1), :], (cells, sides))
                    for f in range(4)
                ],
                axis=0,
            )
            out_ref[i, j] = center_ref[i, j].astype(F32) + lifted
    for source, start in ((main_near, half * (1 - p)), (main_far, half * p)):
        for i in range(half):
            for j in range(columns):
                out_ref[start + i, j] += source[i, j].astype(F32)
    for source, start in ((cross_near, (columns - 2) * (1 - q)), (cross_far, (columns - 2) * q)):
        for i in range(rows):
            for j in range(2):
                out_ref[i, start + j] += source[i, j].astype(F32)
    for source, start in (
        (corner_near, (columns - 2) * (1 - q)), (corner_far, (columns - 2) * q)
    ):
        for i in range(half):
            for j in range(2):
                out_ref[half * p + i, start + j] += source[i, j].astype(F32)
    for i in range(rows):
        for j in range(columns):

            @pl.when(i * columns + j >= info_ref[0])
            def _(i=i, j=j):
                out_ref[i, j] = jnp.zeros((width, sides), F32)


def join(info, lifted, center, pieces):
    return call(
        join_kernel, "join", shaped(center.shape, F32), (info, lifted, center) + pieces,
        [SMEM] + [VMEM] * 8, VMEM, 6, flops=8 * center.size, moved=10 * center.size,
    )


def body(residual, approx_inverse, pattern, live_blocks, block_aggregate, coarse_inverse):
    rows, columns = residual.shape[:2]
    info = jnp.stack([live_blocks[0, 0], lax.axis_index("stream"), lax.axis_index("cross")])
    own_near, own_far, edge_near, edge_far, corner_near, corner_far = mask_blocks(info, residual)
    slots, size = lax.axis_size("stream") // 2, coarse_inverse.shape[0]
    parts = partial_sums(info, block_aggregate, own_near, own_far, slots, size)
    got_far = swap_far(own_far, "stream")
    cross_far = swap_far(edge_far, "cross")
    cross_near = swap_near(edge_near, "cross")
    corner_near = swap_diagonal(corner_near, lambda j: j ^ 1)
    corner_far = swap_diagonal(corner_far, far_of)
    blocks, links = approx_inverse[0], jnp.transpose(pattern[0])
    blocks, parts = lax.optimization_barrier((blocks, parts))
    blocks = jnp.where(info[0] > 0, blocks, jnp.zeros((), BF16))
    parts = exchange_in_half(parts, "stream")
    own_sums = half_sums(parts, coarse_inverse)
    got_far, cross_far, cross_near, blocks, own_sums = lax.optimization_barrier(
        (got_far, cross_far, cross_near, blocks, own_sums)
    )
    other_sums = swap_halves(own_sums, "stream")
    got_near = swap_near(near_message(info, own_near, cross_near, cross_far), "stream")
    got_near, other_sums = lax.optimization_barrier((got_near, other_sums))
    pieces = (
        own_near, own_far, got_near, got_far, cross_near, cross_far, corner_near, corner_far
    )
    near, far, corner_near, corner_far, grid = margin_fixes(info, links, blocks, pieces)
    far, near, other_sums = lax.optimization_barrier((far, near, other_sums))
    far = swap_far(far, "stream")
    near = swap_near(near, "stream")
    side_near, side_far, center = center_fixes(info, links, blocks, grid, rows, columns)
    side_near, side_far = fold_sides(info, side_near, side_far, near)
    cross_far = swap_far(side_far, "cross")
    cross_near = swap_near(side_near, "cross")
    corner_near = swap_diagonal(corner_near, lambda j: j ^ 1)
    corner_far = swap_diagonal(corner_far, far_of)
    coarse = coarse_solve(info, own_sums, other_sums, slots, size)
    lifted = lift(block_aggregate, exchange_in_half(coarse, "stream"))
    pieces = (near, far, cross_near, cross_far, corner_near, corner_far)
    return join(info, lifted, center, pieces)


def solution(mesh):
    placed = (
        P("stream", "cross", None, None),
        P("stream", "cross", None, None),
        P("stream", "cross", None),
        P("stream", "cross"),
        P("stream", "cross"),
        P("stream", "cross"),
    )
    return jax.shard_map(
        body,
        mesh=mesh,
        in_specs=placed,
        out_specs=P("stream", "cross", None, None),
        check_vma=False,
    )
```

```python
import jax
import jax.numpy as jnp
from jax import lax
from jax.experimental import pallas as pl
from jax.experimental.pallas import tpu as pltpu
from jax.sharding import PartitionSpec as P

BF16 = jnp.bfloat16
F32 = jnp.float32
MIB = 1 << 20
HOLD = 1 << 34
VMEM = pl.BlockSpec(memory_space=pltpu.VMEM)
SMEM = pl.BlockSpec(memory_space=pltpu.SMEM)


def swap_near(values, axis):
    count = lax.axis_size(axis)
    return lax.ppermute(values, axis, [(i, i ^ 1) for i in range(count) if i ^ 1 < count])


def swap_far(values, axis):
    count = lax.axis_size(axis)
    pairs = []
    for i in range(1, count - 1, 2):
        pairs += [(i, i + 1), (i + 1, i)]
    return lax.ppermute(values, axis, pairs)


def swap_bit(values, axis, bit):
    count = lax.axis_size(axis)
    return lax.ppermute(values, axis, [(i, i ^ bit) for i in range(count)])


def shaped(shape, dtype):
    return jax.ShapeDtypeStruct(shape, dtype)


def call(kernel, name, outs, ins, specs, out_specs, limit, flops=HOLD, scratch=()):
    return pl.pallas_call(
        kernel,
        out_shape=outs,
        in_specs=specs,
        out_specs=out_specs,
        scratch_shapes=list(scratch),
        cost_estimate=pl.CostEstimate(flops=flops, bytes_accessed=1024, transcendentals=0),
        compiler_params=pltpu.CompilerParams(vmem_limit_bytes=limit * MIB),
        name=name,
    )(*ins)


def parities(info_ref):
    return info_ref[1] % 2, info_ref[2] % 2


def mask_kernel(info_ref, residual_ref, near_ref, far_ref, cross_near, cross_far):
    rows, columns = residual_ref.shape[:2]
    half = rows // 2
    p, q = parities(info_ref)
    for out_ref, start in ((near_ref, half * (1 - p)), (far_ref, half * p)):
        for i in range(half):
            for j in range(columns):
                block = residual_ref[start + i, j]
                live = (start + i) * columns + j < info_ref[0]
                out_ref[i, j] = jnp.where(live, block, jnp.zeros_like(block))
    for out_ref, start in ((cross_near, (columns - 2) * (1 - q)), (cross_far, (columns - 2) * q)):
        for i in range(rows):
            for j in range(2):
                block = residual_ref[i, start + j]
                live = i * columns + start + j < info_ref[0]
                out_ref[i, j] = jnp.where(live, block, jnp.zeros_like(block))


def mask_blocks(info, residual):
    rows, columns, width, sides = residual.shape
    wide = shaped((rows // 2, columns, width, sides), BF16)
    tall = shaped((rows, 2, width, sides), BF16)
    return call(
        mask_kernel, "mask_blocks", (wide, wide, tall, tall), (info, residual),
        [SMEM, VMEM], (VMEM,) * 4, 4,
    )


def payload_kernel(info_ref, agg_ref, near_ref, far_ref, inverse_ref, out_ref):
    unknowns, sides = near_ref.shape
    rows, columns = agg_ref.shape
    half = rows * columns * 2
    size = inverse_ref.shape[0]
    cells = unknowns // half
    p, _ = parities(info_ref)
    row = lax.broadcasted_iota(jnp.int32, (half, unknowns), 0)
    column = lax.broadcasted_iota(jnp.int32, (half, unknowns), 1)
    picks = jnp.where(column // cells == row, 1.0, 0.0).astype(BF16)
    for source, start in ((near_ref, half * (1 - p)), (far_ref, half * p)):
        sums = jnp.dot(picks, source[...], preferred_element_type=F32)
        out_ref[pl.ds(pl.multiple_of(start, half), half), :] = sums.astype(BF16)
    row = lax.broadcasted_iota(jnp.int32, (size, sides), 0)
    column = lax.broadcasted_iota(jnp.int32, (size, sides), 1)
    rest = inverse_ref[...]
    tail = jnp.zeros((size, sides), F32)
    for term in range(3):
        part = rest.astype(BF16)
        rest = rest - part.astype(F32)
        place = jnp.where(column == row + term * size, 1.0, 0.0).astype(BF16)
        tail = tail + jnp.dot(part, place, preferred_element_type=F32)
    lane = lax.broadcasted_iota(jnp.int32, (1, sides), 1) - 3 * size
    labels = jnp.zeros((1, sides), F32)
    for i in range(rows):
        for j in range(columns):
            labels = jnp.where(lane == i * columns + j, agg_ref[i, j].astype(F32), labels)
    out_ref[pl.ds(2 * half, size), :] = (tail + labels).astype(BF16)


def payload_of(info, agg, near, far, inverse):
    sides = near.shape[-1]
    rows, columns = agg.shape
    flat = (near.size // sides, sides)
    count = rows * columns * 4 + inverse.shape[0]
    return call(
        payload_kernel, "payload", shaped((1, count, sides), BF16),
        (info, agg, near.reshape(flat), far.reshape(flat), inverse),
        [SMEM, SMEM, VMEM, VMEM, VMEM], pl.BlockSpec((None, count, sides), lambda: (0, 0, 0)),
        6,
    )


def join_pair_kernel(first_ref, second_ref, out_ref):
    count = first_ref.shape[0]
    out_ref[:count] = first_ref[...]
    out_ref[count:] = second_ref[...]


def join_pair(first, second):
    count = first.shape[0]
    return call(
        join_pair_kernel, "join_pair", shaped((2 * count,) + first.shape[1:], BF16),
        (first, second), [VMEM, VMEM], VMEM, 3,
    )


def corners_kernel(info_ref, own_near, cross_near, cross_far, near_ref, far_ref):
    half, columns = own_near.shape[:2]
    p, _ = parities(info_ref)
    for i in range(half):
        for j in range(columns):
            near_ref[i, j] = own_near[i, j]
    for out_ref, start, base in ((near_ref, half * (1 - p), columns), (far_ref, half * p, 0)):
        for i in range(half):
            for j in range(2):
                out_ref[i, base + j] = cross_near[start + i, j]
                out_ref[i, base + 2 + j] = cross_far[start + i, j]


def corners(info, own_near, cross_near, cross_far):
    half, columns, width, sides = own_near.shape
    return call(
        corners_kernel, "corners",
        (shaped((half, columns + 4, width, sides), BF16), shaped((half, 4, width, sides), BF16)),
        (info, own_near, cross_near, cross_far), [SMEM, VMEM, VMEM, VMEM], (VMEM, VMEM), 3,
    )


def fix_of(pattern_ref, blocks_ref, grid_ref, n):
    picked = jnp.concatenate([grid_ref[pattern_ref[k, n]] for k in range(4)], axis=0)
    return jnp.dot(blocks_ref[n], picked, preferred_element_type=F32).astype(BF16)


def margin_kernel(
    info_ref, pattern_ref, blocks_ref,
    own_near, own_far, got_near, got_far, cross_near, cross_far, corner_far,
    out_near, main_far, out_far, grid_ref,
):
    half, columns = own_near.shape[:2]
    rows = 2 * half
    wide = columns + 4
    p, q = parities(info_ref)
    near_row, far_row = (rows + 2) * (1 - p), (rows + 2) * p
    near_column, far_column = (columns + 2) * (1 - q), (columns + 2) * q
    for source, start in (
        (own_near, 2 + half * (1 - p)), (own_far, 2 + half * p),
        (got_near, near_row), (got_far, far_row),
    ):
        for i in range(2):
            for j in range(columns):
                grid_ref[(start + i) * wide + 2 + j] = source[i, j]
    for source, start in ((cross_near, near_column), (cross_far, far_column)):
        for i in range(rows):
            for j in range(2):
                grid_ref[(2 + i) * wide + start + j] = source[i, j]
    for source, start, first in ((got_near, near_row, columns), (corner_far, far_row, 0)):
        for i in range(2):
            for j in range(2):
                grid_ref[(start + i) * wide + near_column + j] = source[i, first + j]
                grid_ref[(start + i) * wide + far_column + j] = source[i, first + 2 + j]
    for main, corner, first, start in (
        (main_far, out_far, 0, far_row), (out_near, out_near, columns, near_row)
    ):
        for i in range(2):
            base = (start + i) * wide
            for j in range(2):
                corner[i, first + j] = fix_of(
                    pattern_ref, blocks_ref, grid_ref, base + near_column + j
                )
                corner[i, first + 2 + j] = fix_of(
                    pattern_ref, blocks_ref, grid_ref, base + far_column + j
                )
            for j in range(columns):
                main[i, j] = fix_of(pattern_ref, blocks_ref, grid_ref, base + 2 + j)


def margin_fixes(info, pattern, blocks, pieces):
    count, width, depth = blocks.shape
    half, columns, _, sides = pieces[0].shape
    near = shaped((2, columns + 4, width, sides), BF16)
    main = shaped((2, columns, width, sides), BF16)
    corner = shaped((2, 4, width, sides), BF16)
    grid = shaped((count, width, sides), BF16)
    return call(
        margin_kernel, "margin_fixes", (near, main, corner, grid),
        (info, pattern, blocks) + pieces, [SMEM, SMEM] + [VMEM] * 8, (VMEM,) * 4, 12,
    )


def center_kernel(info_ref, pattern_ref, blocks_ref, grid_ref, side_near, side_far, center_ref):
    rows, columns = center_ref.shape[:2]
    wide = columns + 4
    _, q = parities(info_ref)
    near_column, far_column = (columns + 2) * (1 - q), (columns + 2) * q
    for i in range(rows):
        base = (2 + i) * wide
        for j in range(2):
            side_near[i, j] = fix_of(pattern_ref, blocks_ref, grid_ref, base + near_column + j)
            side_far[i, j] = fix_of(pattern_ref, blocks_ref, grid_ref, base + far_column + j)
        for j in range(columns):
            center_ref[i, j] = fix_of(pattern_ref, blocks_ref, grid_ref, base + 2 + j)


def center_fixes(info, pattern, blocks, grid, rows, columns):
    _, width, sides = grid.shape
    side = shaped((rows, 2, width, sides), BF16)
    return call(
        center_kernel, "center_fixes",
        (side, side, shaped((rows, columns, width, sides), BF16)),
        (info, pattern, blocks, grid), [SMEM, SMEM, VMEM, VMEM], (VMEM,) * 3, 12, flops=0,
    )


def fold_kernel(info_ref, side_near, side_far, got_near, corner_far, out_near, out_far):
    half, wide = got_near.shape[:2]
    p, _ = parities(info_ref)
    for source, start, first in (
        (got_near, half * (1 - p), wide - 4), (corner_far, half * p, 0)
    ):
        for i in range(half):
            for j in range(2):
                for side, out, at in ((side_near, out_near, j), (side_far, out_far, 2 + j)):
                    total = side[start + i, j].astype(F32) + source[i, first + at].astype(F32)
                    out[start + i, j] = total.astype(BF16)


def fold_sides(info, side_near, side_far, got_near, corner_far):
    piece = shaped(side_near.shape, BF16)
    return call(
        fold_kernel, "fold_sides", (piece, piece),
        (info, side_near, side_far, got_near, corner_far),
        [SMEM] + [VMEM] * 4, (VMEM, VMEM), 3,
    )


def split_dot(left, right):
    high = right.astype(BF16)
    low = (right - high.astype(F32)).astype(BF16)
    return jnp.dot(left, high, preferred_element_type=F32) + jnp.dot(
        left, low, preferred_element_type=F32
    )


def solve_kernel(bits, info_ref, agg_ref, first_ref, second_ref, out_ref, sums, coarse):
    count, height, sides = first_ref.shape
    rows, columns = agg_ref.shape
    fields = rows * columns * 4
    size = height - fields
    total = sums.shape[0]
    row = lax.broadcasted_iota(jnp.int32, (sides, fields), 0)
    column = lax.broadcasted_iota(jnp.int32, (sides, fields), 1)
    repeat = jnp.where(row - 3 * size == column // 4, 1.0, 0.0).astype(BF16)
    row = lax.broadcasted_iota(jnp.int32, (total, fields), 0)
    column = lax.broadcasted_iota(jnp.int32, (total, fields), 1)
    same_field = row % 4 == column % 4
    owner = (row // 4).astype(F32)
    for part, source in enumerate((first_ref, second_ref)):
        for k in range(count):
            tail = source[k, pl.ds(fields, 16), :]
            labels = jnp.dot(tail, repeat, preferred_element_type=F32)[:1]
            onehot = jnp.where(same_field & (owner == labels), 1.0, 0.0).astype(BF16)
            found = jnp.dot(
                onehot, source[k, pl.ds(0, fields), :], preferred_element_type=F32
            )
            if part == 0 and k == 0:
                sums[...] = found
            else:
                sums[...] += found
    for part, source in enumerate((first_ref, second_ref)):
        for k in range(count):
            slot, flips = part * count + k, 0
            for i, bit in enumerate(bits):
                if slot >> i & 1:
                    flips |= bit
            start = pl.multiple_of((info_ref[1] ^ flips) * size, size)
            mine = sums[pl.ds(start, size), :]
            stacked = jnp.concatenate([mine, mine, mine, jnp.zeros_like(mine)], axis=0)
            coarse[pl.ds(start, size), :] = split_dot(
                source[k, pl.ds(fields, size), :], stacked
            )
    row = lax.broadcasted_iota(jnp.int32, (fields, 1), 0)
    labels = jnp.zeros((fields, 1), jnp.int32)
    for i in range(rows):
        for j in range(columns):
            labels = jnp.where(row // 4 == i * columns + j, agg_ref[i, j], labels)
    row = lax.broadcasted_iota(jnp.int32, (fields, total), 0)
    column = lax.broadcasted_iota(jnp.int32, (fields, total), 1)
    onehot = jnp.where((column // 4 == labels) & (column % 4 == row % 4), 1.0, 0.0)
    out_ref[...] = split_dot(onehot.astype(BF16), coarse[...])


def coarse_values(bits, info, agg, first, second):
    count, height, sides = first.shape
    fields = agg.size * 4
    total = 2 * count * (height - fields)

    def kernel(*refs):
        solve_kernel(bits, *refs)

    return call(
        kernel, "coarse_values", shaped((fields, sides), F32), (info, agg, first, second),
        [SMEM, SMEM, VMEM, VMEM], VMEM, 8,
        scratch=[pltpu.VMEM((total, sides), F32), pltpu.VMEM((total, sides), F32)],
    )


def join_kernel(
    info_ref, lifted_ref, center_ref, main_near, main_far, cross_near, cross_far, out_ref
):
    rows, columns, width, sides = center_ref.shape
    half = rows // 2
    cells = width // 4
    p, q = parities(info_ref)
    for i in range(rows):
        for j in range(columns):
            block = i * columns + j
            lifted = jnp.concatenate(
                [
                    jnp.broadcast_to(lifted_ref[pl.ds(block * 4 + f, 1), :], (cells, sides))
                    for f in range(4)
                ],
                axis=0,
            )
            out_ref[i, j] = center_ref[i, j].astype(F32) + lifted
    for source, start in ((main_near, half * (1 - p)), (main_far, half * p)):
        for i in range(half):
            for j in range(columns):
                out_ref[start + i, j] += source[i, j].astype(F32)
    for source, start in ((cross_near, (columns - 2) * (1 - q)), (cross_far, (columns - 2) * q)):
        for i in range(rows):
            for j in range(2):
                out_ref[i, start + j] += source[i, j].astype(F32)
    for i in range(rows):
        for j in range(columns):

            @pl.when(i * columns + j >= info_ref[0])
            def _(i=i, j=j):
                out_ref[i, j] = jnp.zeros((width, sides), F32)


def join(info, lifted, center, main_near, main_far, cross_near, cross_far):
    return call(
        join_kernel, "join", shaped(center.shape, F32),
        (info, lifted, center, main_near, main_far, cross_near, cross_far),
        [SMEM] + [VMEM] * 6, VMEM, 6,
    )


def body(residual, approx_inverse, pattern, live_blocks, block_aggregate, coarse_inverse):
    rows, columns = residual.shape[:2]
    info = jnp.stack([live_blocks[0, 0], lax.axis_index("stream"), lax.axis_index("cross")])
    own_near, own_far, edge_near, edge_far = mask_blocks(info, residual)
    bits = []
    while 2 << len(bits) <= lax.axis_size("stream"):
        bits.insert(0, 1 << len(bits))
    gathered = payload_of(info, block_aggregate, own_near, own_far, coarse_inverse)
    got_far = swap_far(own_far, "stream")
    cross_far = swap_far(edge_far, "cross")
    cross_near = swap_near(edge_near, "cross")
    blocks, links = approx_inverse[0], jnp.transpose(pattern[0])
    got_far, cross_far, cross_near, gathered = lax.optimization_barrier(
        (got_far, cross_far, cross_near, gathered)
    )
    other = swap_bit(gathered, "stream", bits[0])
    got_near, corner_far = corners(info, own_near, cross_near, cross_far)
    corner_far = swap_far(corner_far, "stream")
    got_near = swap_near(got_near, "stream")
    gathered = join_pair(gathered, other)
    other = swap_bit(gathered, "stream", bits[1])
    gathered, corner_far, got_near = lax.optimization_barrier((gathered, corner_far, got_near))
    pieces = (own_near, own_far, got_near, got_far, cross_near, cross_far, corner_far)
    near, far, corner_far, grid = margin_fixes(info, links, blocks, pieces)
    corner_far, other = lax.optimization_barrier((corner_far, other))
    corner_far = swap_far(corner_far, "stream")
    near = swap_near(near, "stream")
    far = swap_far(far, "stream")
    if bits[2:]:
        gathered = join_pair(gathered, other)
        other = swap_bit(gathered, "stream", bits[2])
    near, grid = lax.optimization_barrier((near, grid))
    side_near, side_far, center = center_fixes(info, links, blocks, grid, rows, columns)
    side_near, other = lax.optimization_barrier((side_near, other))
    for bit in bits[3:]:
        gathered = join_pair(gathered, other)
        other = swap_bit(gathered, "stream", bit)
    gathered, near, corner_far = lax.optimization_barrier((gathered, near, corner_far))
    side_near, side_far = fold_sides(info, side_near, side_far, near, corner_far)
    cross_far = swap_far(side_far, "cross")
    cross_near = swap_near(side_near, "cross")
    lifted = coarse_values(bits, info, block_aggregate, gathered, other)
    return join(info, lifted, center, near, far, cross_near, cross_far)


def solution(mesh):
    placed = (
        P("stream", "cross", None, None),
        P("stream", "cross", None, None),
        P("stream", "cross", None),
        P("stream", "cross"),
        P("stream", "cross"),
        P("stream", "cross"),
    )
    return jax.shard_map(
        body,
        mesh=mesh,
        in_specs=placed,
        out_specs=P("stream", "cross", None, None),
        check_vma=False,
    )
```

```python
import jax
import jax.numpy as jnp
from jax import lax
from jax.experimental import pallas as pl
from jax.experimental.pallas import tpu as pltpu
from jax.sharding import PartitionSpec as P

BF16 = jnp.bfloat16
F32 = jnp.float32
MIB = 1 << 20
HOLD = 1 << 34
VMEM = pl.BlockSpec(memory_space=pltpu.VMEM)
SMEM = pl.BlockSpec(memory_space=pltpu.SMEM)


def swap_near(values, axis):
    count = lax.axis_size(axis)
    return lax.ppermute(values, axis, [(i, i ^ 1) for i in range(count) if i ^ 1 < count])


def swap_far(values, axis):
    count = lax.axis_size(axis)
    pairs = []
    for i in range(1, count - 1, 2):
        pairs += [(i, i + 1), (i + 1, i)]
    return lax.ppermute(values, axis, pairs)


def swap_bit(values, axis, bit):
    count = lax.axis_size(axis)
    return lax.ppermute(values, axis, [(i, i ^ bit) for i in range(count)])


def shaped(shape, dtype):
    return jax.ShapeDtypeStruct(shape, dtype)


def call(kernel, name, outs, ins, specs, out_specs, limit, flops=HOLD, scratch=()):
    return pl.pallas_call(
        kernel,
        out_shape=outs,
        in_specs=specs,
        out_specs=out_specs,
        scratch_shapes=list(scratch),
        cost_estimate=pl.CostEstimate(flops=flops, bytes_accessed=1024, transcendentals=0),
        compiler_params=pltpu.CompilerParams(vmem_limit_bytes=limit * MIB),
        name=name,
    )(*ins)


def parities(info_ref):
    return info_ref[1] % 2, info_ref[2] % 2


def mask_kernel(info_ref, residual_ref, near_ref, far_ref, cross_near, cross_far):
    rows, columns = residual_ref.shape[:2]
    half = rows // 2
    p, q = parities(info_ref)
    for out_ref, start in ((near_ref, half * (1 - p)), (far_ref, half * p)):
        for i in range(half):
            for j in range(columns):
                block = residual_ref[start + i, j]
                live = (start + i) * columns + j < info_ref[0]
                out_ref[i, j] = jnp.where(live, block, jnp.zeros_like(block))
    for out_ref, start in ((cross_near, (columns - 2) * (1 - q)), (cross_far, (columns - 2) * q)):
        for i in range(rows):
            for j in range(2):
                block = residual_ref[i, start + j]
                live = i * columns + start + j < info_ref[0]
                out_ref[i, j] = jnp.where(live, block, jnp.zeros_like(block))


def mask_blocks(info, residual):
    rows, columns, width, sides = residual.shape
    wide = shaped((rows // 2, columns, width, sides), BF16)
    tall = shaped((rows, 2, width, sides), BF16)
    return call(
        mask_kernel, "mask_blocks", (wide, wide, tall, tall), (info, residual),
        [SMEM, VMEM], (VMEM,) * 4, 4,
    )


def payload_kernel(info_ref, agg_ref, near_ref, far_ref, inverse_ref, out_ref):
    unknowns, sides = near_ref.shape
    rows, columns = agg_ref.shape
    half = rows * columns * 2
    size = inverse_ref.shape[0]
    cells = unknowns // half
    p, _ = parities(info_ref)
    row = lax.broadcasted_iota(jnp.int32, (half, unknowns), 0)
    column = lax.broadcasted_iota(jnp.int32, (half, unknowns), 1)
    picks = jnp.where(column // cells == row, 1.0, 0.0).astype(BF16)
    for source, start in ((near_ref, half * (1 - p)), (far_ref, half * p)):
        sums = jnp.dot(picks, source[...], preferred_element_type=F32)
        out_ref[pl.ds(pl.multiple_of(start, half), half), :] = sums.astype(BF16)
    row = lax.broadcasted_iota(jnp.int32, (size, sides), 0)
    column = lax.broadcasted_iota(jnp.int32, (size, sides), 1)
    rest = inverse_ref[...]
    tail = jnp.zeros((size, sides), F32)
    for term in range(3):
        part = rest.astype(BF16)
        rest = rest - part.astype(F32)
        place = jnp.where(column == row + term * size, 1.0, 0.0).astype(BF16)
        tail = tail + jnp.dot(part, place, preferred_element_type=F32)
    lane = lax.broadcasted_iota(jnp.int32, (1, sides), 1) - 3 * size
    labels = jnp.zeros((1, sides), F32)
    for i in range(rows):
        for j in range(columns):
            labels = jnp.where(lane == i * columns + j, agg_ref[i, j].astype(F32), labels)
    out_ref[pl.ds(2 * half, size), :] = (tail + labels).astype(BF16)


def payload_of(info, agg, near, far, inverse):
    sides = near.shape[-1]
    rows, columns = agg.shape
    flat = (near.size // sides, sides)
    count = rows * columns * 4 + inverse.shape[0]
    return call(
        payload_kernel, "payload", shaped((1, count, sides), BF16),
        (info, agg, near.reshape(flat), far.reshape(flat), inverse),
        [SMEM, SMEM, VMEM, VMEM, VMEM], pl.BlockSpec((None, count, sides), lambda: (0, 0, 0)),
        6,
    )


def join_pair_kernel(first_ref, second_ref, out_ref):
    count = first_ref.shape[0]
    out_ref[:count] = first_ref[...]
    out_ref[count:] = second_ref[...]


def join_pair(first, second):
    count = first.shape[0]
    return call(
        join_pair_kernel, "join_pair", shaped((2 * count,) + first.shape[1:], BF16),
        (first, second), [VMEM, VMEM], VMEM, 3,
    )


def far_corner_kernel(info_ref, cross_near, cross_far, far_ref):
    half = far_ref.shape[0]
    p, _ = parities(info_ref)
    for i in range(half):
        for j in range(2):
            far_ref[i, j] = cross_near[half * p + i, j]
            far_ref[i, 2 + j] = cross_far[half * p + i, j]


def far_corners(info, cross_near, cross_far):
    rows, _, width, sides = cross_near.shape
    return call(
        far_corner_kernel, "far_corners", shaped((rows // 2, 4, width, sides), BF16),
        (info, cross_near, cross_far), [SMEM, VMEM, VMEM], VMEM, 2,
    )


def near_kernel(info_ref, own_near, cross_near, cross_far, near_ref):
    half, columns = own_near.shape[:2]
    p, _ = parities(info_ref)
    start = half * (1 - p)
    for i in range(half):
        for j in range(columns):
            near_ref[i, j] = own_near[i, j]
        for j in range(2):
            near_ref[i, columns + j] = cross_near[start + i, j]
            near_ref[i, columns + 2 + j] = cross_far[start + i, j]


def near_message(info, own_near, cross_near, cross_far):
    half, columns, width, sides = own_near.shape
    return call(
        near_kernel, "near_message", shaped((half, columns + 4, width, sides), BF16),
        (info, own_near, cross_near, cross_far), [SMEM, VMEM, VMEM, VMEM], VMEM, 3,
    )


def fix_of(pattern_ref, blocks_ref, grid_ref, n):
    picked = jnp.concatenate([grid_ref[pattern_ref[k, n]] for k in range(4)], axis=0)
    return jnp.dot(blocks_ref[n], picked, preferred_element_type=F32).astype(BF16)


def far_margin_kernel(
    info_ref, pattern_ref, blocks_ref,
    own_near, own_far, got_near, got_far, cross_near, cross_far, corner_far,
    main_far, out_far, grid_ref,
):
    half, columns = own_near.shape[:2]
    rows = 2 * half
    wide = columns + 4
    p, q = parities(info_ref)
    near_row, far_row = (rows + 2) * (1 - p), (rows + 2) * p
    near_column, far_column = (columns + 2) * (1 - q), (columns + 2) * q
    for source, start in (
        (own_near, 2 + half * (1 - p)), (own_far, 2 + half * p),
        (got_near, near_row), (got_far, far_row),
    ):
        for i in range(2):
            for j in range(columns):
                grid_ref[(start + i) * wide + 2 + j] = source[i, j]
    for source, start in ((cross_near, near_column), (cross_far, far_column)):
        for i in range(rows):
            for j in range(2):
                grid_ref[(2 + i) * wide + start + j] = source[i, j]
    for source, start, first in ((got_near, near_row, columns), (corner_far, far_row, 0)):
        for i in range(2):
            for j in range(2):
                grid_ref[(start + i) * wide + near_column + j] = source[i, first + j]
                grid_ref[(start + i) * wide + far_column + j] = source[i, first + 2 + j]
    for i in range(2):
        base = (far_row + i) * wide
        for j in range(2):
            out_far[i, j] = fix_of(pattern_ref, blocks_ref, grid_ref, base + near_column + j)
            out_far[i, 2 + j] = fix_of(pattern_ref, blocks_ref, grid_ref, base + far_column + j)
        for j in range(columns):
            main_far[i, j] = fix_of(pattern_ref, blocks_ref, grid_ref, base + 2 + j)


def far_margin(info, pattern, blocks, pieces):
    count, width, depth = blocks.shape
    half, columns, _, sides = pieces[0].shape
    main = shaped((2, columns, width, sides), BF16)
    corner = shaped((2, 4, width, sides), BF16)
    grid = shaped((count, width, sides), BF16)
    return call(
        far_margin_kernel, "far_margin", (main, corner, grid),
        (info, pattern, blocks) + pieces, [SMEM, SMEM] + [VMEM] * 8, (VMEM,) * 3, 12,
    )


def near_margin_kernel(info_ref, pattern_ref, blocks_ref, grid_ref, out_near):
    wide = out_near.shape[1]
    columns = wide - 4
    rows = grid_ref.shape[0] // wide - 4
    p, q = parities(info_ref)
    near_row = (rows + 2) * (1 - p)
    near_column, far_column = (columns + 2) * (1 - q), (columns + 2) * q
    for i in range(2):
        base = (near_row + i) * wide
        for j in range(2):
            out_near[i, columns + j] = fix_of(
                pattern_ref, blocks_ref, grid_ref, base + near_column + j
            )
            out_near[i, columns + 2 + j] = fix_of(
                pattern_ref, blocks_ref, grid_ref, base + far_column + j
            )
        for j in range(columns):
            out_near[i, j] = fix_of(pattern_ref, blocks_ref, grid_ref, base + 2 + j)


def near_margin(info, pattern, blocks, grid, columns):
    _, width, sides = grid.shape
    return call(
        near_margin_kernel, "near_margin", shaped((2, columns + 4, width, sides), BF16),
        (info, pattern, blocks, grid), [SMEM, SMEM, VMEM, VMEM], VMEM, 12,
    )


def center_kernel(info_ref, pattern_ref, blocks_ref, grid_ref, side_near, side_far, center_ref):
    rows, columns = center_ref.shape[:2]
    wide = columns + 4
    _, q = parities(info_ref)
    near_column, far_column = (columns + 2) * (1 - q), (columns + 2) * q
    for i in range(rows):
        base = (2 + i) * wide
        for j in range(2):
            side_near[i, j] = fix_of(pattern_ref, blocks_ref, grid_ref, base + near_column + j)
            side_far[i, j] = fix_of(pattern_ref, blocks_ref, grid_ref, base + far_column + j)
        for j in range(columns):
            center_ref[i, j] = fix_of(pattern_ref, blocks_ref, grid_ref, base + 2 + j)


def center_fixes(info, pattern, blocks, grid, rows, columns):
    _, width, sides = grid.shape
    side = shaped((rows, 2, width, sides), BF16)
    return call(
        center_kernel, "center_fixes",
        (side, side, shaped((rows, columns, width, sides), BF16)),
        (info, pattern, blocks, grid), [SMEM, SMEM, VMEM, VMEM], (VMEM,) * 3, 12, flops=0,
    )


def fold_kernel(first, info_ref, side_ref, corner_far, got_near, out_ref):
    half, wide = got_near.shape[:2]
    p, _ = parities(info_ref)
    for source, start, base in ((got_near, half * (1 - p), wide - 4), (corner_far, half * p, 0)):
        for i in range(half):
            for j in range(2):
                total = side_ref[start + i, j].astype(F32)
                total = total + source[i, base + first + j].astype(F32)
                out_ref[start + i, j] = total.astype(BF16)


def fold_side(first, info, side, corner_far, got_near):
    def kernel(*refs):
        fold_kernel(first, *refs)

    return call(
        kernel, "fold_side", shaped(side.shape, BF16), (info, side, corner_far, got_near),
        [SMEM] + [VMEM] * 3, VMEM, 3,
    )


def split_dot(left, right):
    high = right.astype(BF16)
    low = (right - high.astype(F32)).astype(BF16)
    return jnp.dot(left, high, preferred_element_type=F32) + jnp.dot(
        left, low, preferred_element_type=F32
    )


def solve_kernel(bits, info_ref, first_ref, second_ref, coarse, sums):
    count, height, sides = first_ref.shape
    total = sums.shape[0]
    size = total // (2 * count)
    fields = height - size
    row = lax.broadcasted_iota(jnp.int32, (sides, fields), 0)
    column = lax.broadcasted_iota(jnp.int32, (sides, fields), 1)
    repeat = jnp.where(row - 3 * size == column // 4, 1.0, 0.0).astype(BF16)
    row = lax.broadcasted_iota(jnp.int32, (total, fields), 0)
    column = lax.broadcasted_iota(jnp.int32, (total, fields), 1)
    same_field = row % 4 == column % 4
    owner = (row // 4).astype(F32)
    for part, source in enumerate((first_ref, second_ref)):
        for k in range(count):
            tail = source[k, pl.ds(fields, 16), :]
            labels = jnp.dot(tail, repeat, preferred_element_type=F32)[:1]
            onehot = jnp.where(same_field & (owner == labels), 1.0, 0.0).astype(BF16)
            found = jnp.dot(
                onehot, source[k, pl.ds(0, fields), :], preferred_element_type=F32
            )
            if part == 0 and k == 0:
                sums[...] = found
            else:
                sums[...] += found
    for part, source in enumerate((first_ref, second_ref)):
        for k in range(count):
            slot, flips = part * count + k, 0
            for i, bit in enumerate(bits):
                if slot >> i & 1:
                    flips |= bit
            start = pl.multiple_of((info_ref[1] ^ flips) * size, size)
            mine = sums[pl.ds(start, size), :]
            stacked = jnp.concatenate([mine, mine, mine, jnp.zeros_like(mine)], axis=0)
            coarse[pl.ds(start, size), :] = split_dot(
                source[k, pl.ds(fields, size), :], stacked
            )


def lift_kernel(agg_ref, coarse_ref, out_ref):
    total = coarse_ref.shape[0]
    rows, columns = agg_ref.shape
    fields = rows * columns * 4
    row = lax.broadcasted_iota(jnp.int32, (fields, 1), 0)
    labels = jnp.zeros((fields, 1), jnp.int32)
    for i in range(rows):
        for j in range(columns):
            labels = jnp.where(row // 4 == i * columns + j, agg_ref[i, j], labels)
    row = lax.broadcasted_iota(jnp.int32, (fields, total), 0)
    column = lax.broadcasted_iota(jnp.int32, (fields, total), 1)
    onehot = jnp.where((column // 4 == labels) & (column % 4 == row % 4), 1.0, 0.0)
    out_ref[...] = split_dot(onehot.astype(BF16), coarse_ref[...])


def coarse_values(bits, info, size, first, second):
    count, height, sides = first.shape
    total = 2 * count * size

    def kernel(*refs):
        solve_kernel(bits, *refs)

    return call(
        kernel, "coarse_values", shaped((total, sides), F32), (info, first, second),
        [SMEM, VMEM, VMEM], VMEM, 8, scratch=[pltpu.VMEM((total, sides), F32)],
    )


def lift(agg, coarse):
    return call(
        lift_kernel, "lift", shaped((agg.size * 4, coarse.shape[1]), F32), (agg, coarse),
        [SMEM, VMEM], VMEM, 3,
    )


def join_kernel(
    info_ref, lifted_ref, center_ref, main_near, main_far, cross_far, cross_near, out_ref
):
    rows, columns, width, sides = center_ref.shape
    half = rows // 2
    cells = width // 4
    p, q = parities(info_ref)
    for i in range(rows):
        for j in range(columns):
            block = i * columns + j
            lifted = jnp.concatenate(
                [
                    jnp.broadcast_to(lifted_ref[pl.ds(block * 4 + f, 1), :], (cells, sides))
                    for f in range(4)
                ],
                axis=0,
            )
            out_ref[i, j] = center_ref[i, j].astype(F32) + lifted
    for source, start in ((main_near, half * (1 - p)), (main_far, half * p)):
        for i in range(half):
            for j in range(columns):
                out_ref[start + i, j] += source[i, j].astype(F32)
    for source, start in ((cross_near, (columns - 2) * (1 - q)), (cross_far, (columns - 2) * q)):
        for i in range(rows):
            for j in range(2):
                out_ref[i, start + j] += source[i, j].astype(F32)
    for i in range(rows):
        for j in range(columns):

            @pl.when(i * columns + j >= info_ref[0])
            def _(i=i, j=j):
                out_ref[i, j] = jnp.zeros((width, sides), F32)


def join(info, lifted, center, main_near, main_far, cross_far, cross_near):
    return call(
        join_kernel, "join", shaped(center.shape, F32),
        (info, lifted, center, main_near, main_far, cross_far, cross_near),
        [SMEM] + [VMEM] * 6, VMEM, 6,
    )


def body(residual, approx_inverse, pattern, live_blocks, block_aggregate, coarse_inverse):
    rows, columns = residual.shape[:2]
    info = jnp.stack([live_blocks[0, 0], lax.axis_index("stream"), lax.axis_index("cross")])
    own_near, own_far, edge_near, edge_far = mask_blocks(info, residual)
    bits = []
    while 2 << len(bits) <= lax.axis_size("stream"):
        bits.insert(0, 1 << len(bits))
    gathered = payload_of(info, block_aggregate, own_near, own_far, coarse_inverse)
    got_far = swap_far(own_far, "stream")
    cross_far = swap_far(edge_far, "cross")
    cross_near = swap_near(edge_near, "cross")
    blocks, links = approx_inverse[0], jnp.transpose(pattern[0])
    got_far, cross_far, cross_near, gathered = lax.optimization_barrier(
        (got_far, cross_far, cross_near, gathered)
    )
    other = swap_bit(gathered, "stream", bits[0])
    corner_far = far_corners(info, cross_near, cross_far)
    corner_far, own_near = lax.optimization_barrier((corner_far, own_near))
    got_near = near_message(info, own_near, cross_near, cross_far)
    corner_far = swap_far(corner_far, "stream")
    got_near = swap_near(got_near, "stream")
    gathered = join_pair(gathered, other)
    other = swap_bit(gathered, "stream", bits[1])
    gathered, corner_far, got_near = lax.optimization_barrier((gathered, corner_far, got_near))
    pieces = (own_near, own_far, got_near, got_far, cross_near, cross_far, corner_far)
    far, corner_far, grid = far_margin(info, links, blocks, pieces)
    near = near_margin(info, links, blocks, grid, columns)
    corner_far = swap_far(corner_far, "stream")
    near = swap_near(near, "stream")
    far = swap_far(far, "stream")
    side_near, side_far, center = center_fixes(info, links, blocks, grid, rows, columns)
    if bits[2:]:
        gathered = join_pair(gathered, other)
        other = swap_bit(gathered, "stream", bits[2])
    corner_far, other = lax.optimization_barrier((corner_far, other))
    for bit in bits[3:]:
        gathered = join_pair(gathered, other)
        other = swap_bit(gathered, "stream", bit)
    side_near = fold_side(0, info, side_near, corner_far, near)
    side_far, side_near = lax.optimization_barrier((side_far, side_near))
    side_far = fold_side(2, info, side_far, corner_far, near)
    cross_far = swap_far(side_far, "cross")
    cross_near = swap_near(side_near, "cross")
    coarse = coarse_values(bits, info, coarse_inverse.shape[0], gathered, other)
    lifted = lift(block_aggregate, coarse)
    return join(info, lifted, center, near, far, cross_far, cross_near)


def solution(mesh):
    placed = (
        P("stream", "cross", None, None),
        P("stream", "cross", None, None),
        P("stream", "cross", None),
        P("stream", "cross"),
        P("stream", "cross"),
        P("stream", "cross"),
    )
    return jax.shard_map(
        body,
        mesh=mesh,
        in_specs=placed,
        out_specs=P("stream", "cross", None, None),
        check_vma=False,
    )
```

```python
import jax
import jax.numpy as jnp
from jax import lax
from jax.experimental import pallas as pl
from jax.experimental.pallas import tpu as pltpu
from jax.sharding import PartitionSpec as P

BF16 = jnp.bfloat16
F32 = jnp.float32
MIB = 1 << 20
HOLD = 1 << 34
VMEM = pl.BlockSpec(memory_space=pltpu.VMEM)
SMEM = pl.BlockSpec(memory_space=pltpu.SMEM)


def swap_near(values, axis):
    count = lax.axis_size(axis)
    return lax.ppermute(values, axis, [(i, i ^ 1) for i in range(count) if i ^ 1 < count])


def swap_far(values, axis):
    count = lax.axis_size(axis)
    pairs = []
    for i in range(1, count - 1, 2):
        pairs += [(i, i + 1), (i + 1, i)]
    return lax.ppermute(values, axis, pairs)


def swap_bit(values, axis, bit):
    count = lax.axis_size(axis)
    return lax.ppermute(values, axis, [(i, i ^ bit) for i in range(count)])


def shaped(shape, dtype):
    return jax.ShapeDtypeStruct(shape, dtype)


def call(kernel, name, outs, ins, specs, out_specs, limit, flops=HOLD, scratch=()):
    return pl.pallas_call(
        kernel,
        out_shape=outs,
        in_specs=specs,
        out_specs=out_specs,
        scratch_shapes=list(scratch),
        cost_estimate=pl.CostEstimate(flops=flops, bytes_accessed=1024, transcendentals=0),
        compiler_params=pltpu.CompilerParams(vmem_limit_bytes=limit * MIB),
        name=name,
    )(*ins)


def parities(info_ref):
    return info_ref[1] % 2, info_ref[2] % 2


def mask_kernel(info_ref, residual_ref, near_ref, far_ref, cross_near, cross_far):
    rows, columns = residual_ref.shape[:2]
    half = rows // 2
    p, q = parities(info_ref)
    for out_ref, start in ((near_ref, half * (1 - p)), (far_ref, half * p)):
        for i in range(half):
            for j in range(columns):
                block = residual_ref[start + i, j]
                live = (start + i) * columns + j < info_ref[0]
                out_ref[i, j] = jnp.where(live, block, jnp.zeros_like(block))
    for out_ref, start in ((cross_near, (columns - 2) * (1 - q)), (cross_far, (columns - 2) * q)):
        for i in range(rows):
            for j in range(2):
                block = residual_ref[i, start + j]
                live = i * columns + start + j < info_ref[0]
                out_ref[i, j] = jnp.where(live, block, jnp.zeros_like(block))


def mask_blocks(info, residual):
    rows, columns, width, sides = residual.shape
    wide = shaped((rows // 2, columns, width, sides), BF16)
    tall = shaped((rows, 2, width, sides), BF16)
    return call(
        mask_kernel, "mask_blocks", (wide, wide, tall, tall), (info, residual),
        [SMEM, VMEM], (VMEM,) * 4, 4,
    )


def payload_kernel(info_ref, agg_ref, near_ref, far_ref, inverse_ref, out_ref):
    unknowns, sides = near_ref.shape
    rows, columns = agg_ref.shape
    half = rows * columns * 2
    size = inverse_ref.shape[0]
    cells = unknowns // half
    p, _ = parities(info_ref)
    row = lax.broadcasted_iota(jnp.int32, (half, unknowns), 0)
    column = lax.broadcasted_iota(jnp.int32, (half, unknowns), 1)
    picks = jnp.where(column // cells == row, 1.0, 0.0).astype(BF16)
    for source, start in ((near_ref, half * (1 - p)), (far_ref, half * p)):
        sums = jnp.dot(picks, source[...], preferred_element_type=F32)
        out_ref[pl.ds(pl.multiple_of(start, half), half), :] = sums.astype(BF16)
    row = lax.broadcasted_iota(jnp.int32, (size, sides), 0)
    column = lax.broadcasted_iota(jnp.int32, (size, sides), 1)
    rest = inverse_ref[...]
    tail = jnp.zeros((size, sides), F32)
    for term in range(3):
        part = rest.astype(BF16)
        rest = rest - part.astype(F32)
        place = jnp.where(column == row + term * size, 1.0, 0.0).astype(BF16)
        tail = tail + jnp.dot(part, place, preferred_element_type=F32)
    lane = lax.broadcasted_iota(jnp.int32, (1, sides), 1) - 3 * size
    labels = jnp.zeros((1, sides), F32)
    for i in range(rows):
        for j in range(columns):
            labels = jnp.where(lane == i * columns + j, agg_ref[i, j].astype(F32), labels)
    out_ref[pl.ds(2 * half, size), :] = (tail + labels).astype(BF16)


def payload_of(info, agg, near, far, inverse):
    sides = near.shape[-1]
    rows, columns = agg.shape
    flat = (near.size // sides, sides)
    count = rows * columns * 4 + inverse.shape[0]
    return call(
        payload_kernel, "payload", shaped((1, count, sides), BF16),
        (info, agg, near.reshape(flat), far.reshape(flat), inverse),
        [SMEM, SMEM, VMEM, VMEM, VMEM], pl.BlockSpec((None, count, sides), lambda: (0, 0, 0)),
        6,
    )


def join_pair_kernel(first_ref, second_ref, out_ref):
    count = first_ref.shape[0]
    out_ref[:count] = first_ref[...]
    out_ref[count:] = second_ref[...]


def join_pair(first, second):
    count = first.shape[0]
    return call(
        join_pair_kernel, "join_pair", shaped((2 * count,) + first.shape[1:], BF16),
        (first, second), [VMEM, VMEM], VMEM, 3,
    )


def corners_kernel(info_ref, own_near, cross_near, cross_far, near_ref, far_ref):
    half, columns = own_near.shape[:2]
    p, _ = parities(info_ref)
    for i in range(half):
        for j in range(columns):
            near_ref[i, j] = own_near[i, j]
    for out_ref, start, base in ((near_ref, half * (1 - p), columns), (far_ref, half * p, 0)):
        for i in range(half):
            for j in range(2):
                out_ref[i, base + j] = cross_near[start + i, j]
                out_ref[i, base + 2 + j] = cross_far[start + i, j]


def corners(info, own_near, cross_near, cross_far):
    half, columns, width, sides = own_near.shape
    return call(
        corners_kernel, "corners",
        (shaped((half, columns + 4, width, sides), BF16), shaped((half, 4, width, sides), BF16)),
        (info, own_near, cross_near, cross_far), [SMEM, VMEM, VMEM, VMEM], (VMEM, VMEM), 3,
    )


def fix_of(pattern_ref, blocks_ref, grid_ref, n):
    picked = jnp.concatenate([grid_ref[pattern_ref[k, n]] for k in range(4)], axis=0)
    return jnp.dot(blocks_ref[n], picked, preferred_element_type=F32).astype(BF16)


def margin_kernel(
    info_ref, pattern_ref, blocks_ref,
    own_near, own_far, got_near, got_far, cross_near, cross_far, corner_far,
    out_near, main_far, out_far, grid_ref,
):
    half, columns = own_near.shape[:2]
    rows = 2 * half
    wide = columns + 4
    p, q = parities(info_ref)
    near_row, far_row = (rows + 2) * (1 - p), (rows + 2) * p
    near_column, far_column = (columns + 2) * (1 - q), (columns + 2) * q
    for source, start in (
        (own_near, 2 + half * (1 - p)), (own_far, 2 + half * p),
        (got_near, near_row), (got_far, far_row),
    ):
        for i in range(2):
            for j in range(columns):
                grid_ref[(start + i) * wide + 2 + j] = source[i, j]
    for source, start in ((cross_near, near_column), (cross_far, far_column)):
        for i in range(rows):
            for j in range(2):
                grid_ref[(2 + i) * wide + start + j] = source[i, j]
    for source, start, first in ((got_near, near_row, columns), (corner_far, far_row, 0)):
        for i in range(2):
            for j in range(2):
                grid_ref[(start + i) * wide + near_column + j] = source[i, first + j]
                grid_ref[(start + i) * wide + far_column + j] = source[i, first + 2 + j]
    for main, corner, first, start in (
        (main_far, out_far, 0, far_row), (out_near, out_near, columns, near_row)
    ):
        for i in range(2):
            base = (start + i) * wide
            for j in range(2):
                corner[i, first + j] = fix_of(
                    pattern_ref, blocks_ref, grid_ref, base + near_column + j
                )
                corner[i, first + 2 + j] = fix_of(
                    pattern_ref, blocks_ref, grid_ref, base + far_column + j
                )
            for j in range(columns):
                main[i, j] = fix_of(pattern_ref, blocks_ref, grid_ref, base + 2 + j)


def margin_fixes(info, pattern, blocks, pieces):
    count, width, depth = blocks.shape
    half, columns, _, sides = pieces[0].shape
    near = shaped((2, columns + 4, width, sides), BF16)
    main = shaped((2, columns, width, sides), BF16)
    corner = shaped((2, 4, width, sides), BF16)
    grid = shaped((count, width, sides), BF16)
    return call(
        margin_kernel, "margin_fixes", (near, main, corner, grid),
        (info, pattern, blocks) + pieces, [SMEM, SMEM] + [VMEM] * 8, (VMEM,) * 4, 12,
    )


def center_kernel(info_ref, pattern_ref, blocks_ref, grid_ref, side_near, side_far, center_ref):
    rows, columns = center_ref.shape[:2]
    wide = columns + 4
    _, q = parities(info_ref)
    near_column, far_column = (columns + 2) * (1 - q), (columns + 2) * q
    for i in range(rows):
        base = (2 + i) * wide
        for j in range(2):
            side_near[i, j] = fix_of(pattern_ref, blocks_ref, grid_ref, base + near_column + j)
            side_far[i, j] = fix_of(pattern_ref, blocks_ref, grid_ref, base + far_column + j)
        for j in range(columns):
            center_ref[i, j] = fix_of(pattern_ref, blocks_ref, grid_ref, base + 2 + j)


def center_fixes(info, pattern, blocks, grid, rows, columns):
    _, width, sides = grid.shape
    side = shaped((rows, 2, width, sides), BF16)
    return call(
        center_kernel, "center_fixes",
        (side, side, shaped((rows, columns, width, sides), BF16)),
        (info, pattern, blocks, grid), [SMEM, SMEM, VMEM, VMEM], (VMEM,) * 3, 12, flops=0,
    )


def fold_kernel(first, info_ref, side_ref, corner_far, got_near, out_ref):
    half, wide = got_near.shape[:2]
    p, _ = parities(info_ref)
    for source, start, base in ((got_near, half * (1 - p), wide - 4), (corner_far, half * p, 0)):
        for i in range(half):
            for j in range(2):
                total = side_ref[start + i, j].astype(F32)
                total = total + source[i, base + first + j].astype(F32)
                out_ref[start + i, j] = total.astype(BF16)


def fold_side(first, info, side, corner_far, got_near):
    def kernel(*refs):
        fold_kernel(first, *refs)

    return call(
        kernel, "fold_side", shaped(side.shape, BF16), (info, side, corner_far, got_near),
        [SMEM] + [VMEM] * 3, VMEM, 3,
    )


def split_dot(left, right):
    high = right.astype(BF16)
    low = (right - high.astype(F32)).astype(BF16)
    return jnp.dot(left, high, preferred_element_type=F32) + jnp.dot(
        left, low, preferred_element_type=F32
    )


def solve_kernel(bits, info_ref, agg_ref, first_ref, second_ref, out_ref, sums, coarse):
    count, height, sides = first_ref.shape
    rows, columns = agg_ref.shape
    fields = rows * columns * 4
    size = height - fields
    total = sums.shape[0]
    row = lax.broadcasted_iota(jnp.int32, (sides, fields), 0)
    column = lax.broadcasted_iota(jnp.int32, (sides, fields), 1)
    repeat = jnp.where(row - 3 * size == column // 4, 1.0, 0.0).astype(BF16)
    row = lax.broadcasted_iota(jnp.int32, (total, fields), 0)
    column = lax.broadcasted_iota(jnp.int32, (total, fields), 1)
    same_field = row % 4 == column % 4
    owner = (row // 4).astype(F32)
    for part, source in enumerate((first_ref, second_ref)):
        for k in range(count):
            tail = source[k, pl.ds(fields, 16), :]
            labels = jnp.dot(tail, repeat, preferred_element_type=F32)[:1]
            onehot = jnp.where(same_field & (owner == labels), 1.0, 0.0).astype(BF16)
            found = jnp.dot(
                onehot, source[k, pl.ds(0, fields), :], preferred_element_type=F32
            )
            if part == 0 and k == 0:
                sums[...] = found
            else:
                sums[...] += found
    for part, source in enumerate((first_ref, second_ref)):
        for k in range(count):
            slot, flips = part * count + k, 0
            for i, bit in enumerate(bits):
                if slot >> i & 1:
                    flips |= bit
            start = pl.multiple_of((info_ref[1] ^ flips) * size, size)
            mine = sums[pl.ds(start, size), :]
            stacked = jnp.concatenate([mine, mine, mine, jnp.zeros_like(mine)], axis=0)
            coarse[pl.ds(start, size), :] = split_dot(
                source[k, pl.ds(fields, size), :], stacked
            )
    row = lax.broadcasted_iota(jnp.int32, (fields, 1), 0)
    labels = jnp.zeros((fields, 1), jnp.int32)
    for i in range(rows):
        for j in range(columns):
            labels = jnp.where(row // 4 == i * columns + j, agg_ref[i, j], labels)
    row = lax.broadcasted_iota(jnp.int32, (fields, total), 0)
    column = lax.broadcasted_iota(jnp.int32, (fields, total), 1)
    onehot = jnp.where((column // 4 == labels) & (column % 4 == row % 4), 1.0, 0.0)
    out_ref[...] = split_dot(onehot.astype(BF16), coarse[...])


def coarse_values(bits, info, agg, first, second):
    count, height, sides = first.shape
    fields = agg.size * 4
    total = 2 * count * (height - fields)

    def kernel(*refs):
        solve_kernel(bits, *refs)

    return call(
        kernel, "coarse_values", shaped((fields, sides), F32), (info, agg, first, second),
        [SMEM, SMEM, VMEM, VMEM], VMEM, 8,
        scratch=[pltpu.VMEM((total, sides), F32), pltpu.VMEM((total, sides), F32)],
    )


def join_kernel(
    info_ref, lifted_ref, center_ref, main_near, main_far, cross_near, cross_far, out_ref
):
    rows, columns, width, sides = center_ref.shape
    half = rows // 2
    cells = width // 4
    p, q = parities(info_ref)
    for i in range(rows):
        for j in range(columns):
            block = i * columns + j
            lifted = jnp.concatenate(
                [
                    jnp.broadcast_to(lifted_ref[pl.ds(block * 4 + f, 1), :], (cells, sides))
                    for f in range(4)
                ],
                axis=0,
            )
            out_ref[i, j] = center_ref[i, j].astype(F32) + lifted
    for source, start in ((main_near, half * (1 - p)), (main_far, half * p)):
        for i in range(half):
            for j in range(columns):
                out_ref[start + i, j] += source[i, j].astype(F32)
    for source, start in ((cross_near, (columns - 2) * (1 - q)), (cross_far, (columns - 2) * q)):
        for i in range(rows):
            for j in range(2):
                out_ref[i, start + j] += source[i, j].astype(F32)
    for i in range(rows):
        for j in range(columns):

            @pl.when(i * columns + j >= info_ref[0])
            def _(i=i, j=j):
                out_ref[i, j] = jnp.zeros((width, sides), F32)


def join(info, lifted, center, main_near, main_far, cross_near, cross_far):
    return call(
        join_kernel, "join", shaped(center.shape, F32),
        (info, lifted, center, main_near, main_far, cross_near, cross_far),
        [SMEM] + [VMEM] * 6, VMEM, 6,
    )


def body(residual, approx_inverse, pattern, live_blocks, block_aggregate, coarse_inverse):
    rows, columns = residual.shape[:2]
    info = jnp.stack([live_blocks[0, 0], lax.axis_index("stream"), lax.axis_index("cross")])
    own_near, own_far, edge_near, edge_far = mask_blocks(info, residual)
    bits = []
    while 2 << len(bits) <= lax.axis_size("stream"):
        bits.insert(0, 1 << len(bits))
    gathered = payload_of(info, block_aggregate, own_near, own_far, coarse_inverse)
    got_far = swap_far(own_far, "stream")
    cross_far = swap_far(edge_far, "cross")
    cross_near = swap_near(edge_near, "cross")
    blocks, links = approx_inverse[0], jnp.transpose(pattern[0])
    got_far, cross_far, cross_near, gathered = lax.optimization_barrier(
        (got_far, cross_far, cross_near, gathered)
    )
    other = swap_bit(gathered, "stream", bits[0])
    got_near, corner_far = corners(info, own_near, cross_near, cross_far)
    corner_far = swap_far(corner_far, "stream")
    got_near = swap_near(got_near, "stream")
    gathered = join_pair(gathered, other)
    other = swap_bit(gathered, "stream", bits[1])
    gathered, corner_far, got_near = lax.optimization_barrier((gathered, corner_far, got_near))
    pieces = (own_near, own_far, got_near, got_far, cross_near, cross_far, corner_far)
    near, far, corner_far, grid = margin_fixes(info, links, blocks, pieces)
    corner_far, other = lax.optimization_barrier((corner_far, other))
    corner_far = swap_far(corner_far, "stream")
    near = swap_near(near, "stream")
    far = swap_far(far, "stream")
    if bits[2:]:
        gathered = join_pair(gathered, other)
        other = swap_bit(gathered, "stream", bits[2])
    near, grid = lax.optimization_barrier((near, grid))
    side_near, side_far, center = center_fixes(info, links, blocks, grid, rows, columns)
    side_near, other = lax.optimization_barrier((side_near, other))
    for bit in bits[3:]:
        gathered = join_pair(gathered, other)
        other = swap_bit(gathered, "stream", bit)
    gathered, near, corner_far = lax.optimization_barrier((gathered, near, corner_far))
    side_far = fold_side(2, info, side_far, corner_far, near)
    side_far, side_near = lax.optimization_barrier((side_far, side_near))
    side_near = fold_side(0, info, side_near, corner_far, near)
    cross_far = swap_far(side_far, "cross")
    cross_near = swap_near(side_near, "cross")
    lifted = coarse_values(bits, info, block_aggregate, gathered, other)
    return join(info, lifted, center, near, far, cross_near, cross_far)


def solution(mesh):
    placed = (
        P("stream", "cross", None, None),
        P("stream", "cross", None, None),
        P("stream", "cross", None),
        P("stream", "cross"),
        P("stream", "cross"),
        P("stream", "cross"),
    )
    return jax.shard_map(
        body,
        mesh=mesh,
        in_specs=placed,
        out_specs=P("stream", "cross", None, None),
        check_vma=False,
    )
```

```python
import jax
import jax.numpy as jnp
from jax import lax
from jax.experimental import pallas as pl
from jax.experimental.pallas import tpu as pltpu
from jax.sharding import PartitionSpec as P

BF16 = jnp.bfloat16
F32 = jnp.float32
MIB = 1 << 20
HOLD = 1 << 34
VMEM = pl.BlockSpec(memory_space=pltpu.VMEM)
SMEM = pl.BlockSpec(memory_space=pltpu.SMEM)


def swap_near(values, axis):
    count = lax.axis_size(axis)
    return lax.ppermute(values, axis, [(i, i ^ 1) for i in range(count) if i ^ 1 < count])


def swap_far(values, axis):
    count = lax.axis_size(axis)
    pairs = []
    for i in range(1, count - 1, 2):
        pairs += [(i, i + 1), (i + 1, i)]
    return lax.ppermute(values, axis, pairs)


def swap_bit(values, axis, bit):
    count = lax.axis_size(axis)
    return lax.ppermute(values, axis, [(i, i ^ bit) for i in range(count)])


def shaped(shape, dtype):
    return jax.ShapeDtypeStruct(shape, dtype)


def call(kernel, name, outs, ins, specs, out_specs, limit, flops=HOLD, scratch=()):
    return pl.pallas_call(
        kernel,
        out_shape=outs,
        in_specs=specs,
        out_specs=out_specs,
        scratch_shapes=list(scratch),
        cost_estimate=pl.CostEstimate(flops=flops, bytes_accessed=1024, transcendentals=0),
        compiler_params=pltpu.CompilerParams(vmem_limit_bytes=limit * MIB),
        name=name,
    )(*ins)


def parities(info_ref):
    return info_ref[1] % 2, info_ref[2] % 2


def mask_kernel(info_ref, residual_ref, near_ref, far_ref, cross_near, cross_far):
    rows, columns = residual_ref.shape[:2]
    half = rows // 2
    p, q = parities(info_ref)
    for out_ref, start in ((near_ref, half * (1 - p)), (far_ref, half * p)):
        for i in range(half):
            for j in range(columns):
                block = residual_ref[start + i, j]
                live = (start + i) * columns + j < info_ref[0]
                out_ref[i, j] = jnp.where(live, block, jnp.zeros_like(block))
    for out_ref, start in ((cross_near, (columns - 2) * (1 - q)), (cross_far, (columns - 2) * q)):
        for i in range(rows):
            for j in range(2):
                block = residual_ref[i, start + j]
                live = i * columns + start + j < info_ref[0]
                out_ref[i, j] = jnp.where(live, block, jnp.zeros_like(block))


def mask_blocks(info, residual):
    rows, columns, width, sides = residual.shape
    wide = shaped((rows // 2, columns, width, sides), BF16)
    tall = shaped((rows, 2, width, sides), BF16)
    return call(
        mask_kernel, "mask_blocks", (wide, wide, tall, tall), (info, residual),
        [SMEM, VMEM], (VMEM,) * 4, 4,
    )


def payload_kernel(info_ref, agg_ref, near_ref, far_ref, inverse_ref, out_ref):
    unknowns, sides = near_ref.shape
    rows, columns = agg_ref.shape
    half = rows * columns * 2
    size = inverse_ref.shape[0]
    cells = unknowns // half
    p, _ = parities(info_ref)
    row = lax.broadcasted_iota(jnp.int32, (half, unknowns), 0)
    column = lax.broadcasted_iota(jnp.int32, (half, unknowns), 1)
    picks = jnp.where(column // cells == row, 1.0, 0.0).astype(BF16)
    for source, start in ((near_ref, half * (1 - p)), (far_ref, half * p)):
        sums = jnp.dot(picks, source[...], preferred_element_type=F32)
        out_ref[pl.ds(pl.multiple_of(start, half), half), :] = sums.astype(BF16)
    row = lax.broadcasted_iota(jnp.int32, (size, sides), 0)
    column = lax.broadcasted_iota(jnp.int32, (size, sides), 1)
    rest = inverse_ref[...]
    tail = jnp.zeros((size, sides), F32)
    for term in range(3):
        part = rest.astype(BF16)
        rest = rest - part.astype(F32)
        place = jnp.where(column == row + term * size, 1.0, 0.0).astype(BF16)
        tail = tail + jnp.dot(part, place, preferred_element_type=F32)
    lane = lax.broadcasted_iota(jnp.int32, (1, sides), 1) - 3 * size
    labels = jnp.zeros((1, sides), F32)
    for i in range(rows):
        for j in range(columns):
            labels = jnp.where(lane == i * columns + j, agg_ref[i, j].astype(F32), labels)
    out_ref[pl.ds(2 * half, size), :] = (tail + labels).astype(BF16)


def payload_of(info, agg, near, far, inverse):
    sides = near.shape[-1]
    rows, columns = agg.shape
    flat = (near.size // sides, sides)
    count = rows * columns * 4 + inverse.shape[0]
    return call(
        payload_kernel, "payload", shaped((1, count, sides), BF16),
        (info, agg, near.reshape(flat), far.reshape(flat), inverse),
        [SMEM, SMEM, VMEM, VMEM, VMEM], pl.BlockSpec((None, count, sides), lambda: (0, 0, 0)),
        6,
    )


def join_pair_kernel(first_ref, second_ref, out_ref):
    count = first_ref.shape[0]
    out_ref[:count] = first_ref[...]
    out_ref[count:] = second_ref[...]


def join_pair(first, second):
    count = first.shape[0]
    return call(
        join_pair_kernel, "join_pair", shaped((2 * count,) + first.shape[1:], BF16),
        (first, second), [VMEM, VMEM], VMEM, 3,
    )


def corners_kernel(info_ref, own_near, cross_near, cross_far, near_ref, far_ref):
    half, columns = own_near.shape[:2]
    p, _ = parities(info_ref)
    for i in range(half):
        for j in range(columns):
            near_ref[i, j] = own_near[i, j]
    for out_ref, start, base in ((near_ref, half * (1 - p), columns), (far_ref, half * p, 0)):
        for i in range(half):
            for j in range(2):
                out_ref[i, base + j] = cross_near[start + i, j]
                out_ref[i, base + 2 + j] = cross_far[start + i, j]


def corners(info, own_near, cross_near, cross_far):
    half, columns, width, sides = own_near.shape
    return call(
        corners_kernel, "corners",
        (shaped((half, columns + 4, width, sides), BF16), shaped((half, 4, width, sides), BF16)),
        (info, own_near, cross_near, cross_far), [SMEM, VMEM, VMEM, VMEM], (VMEM, VMEM), 3,
    )


def fix_of(pattern_ref, blocks_ref, grid_ref, n):
    picked = jnp.concatenate([grid_ref[pattern_ref[k, n]] for k in range(4)], axis=0)
    return jnp.dot(blocks_ref[n], picked, preferred_element_type=F32).astype(BF16)


def margin_kernel(
    info_ref, pattern_ref, blocks_ref,
    own_near, own_far, got_near, got_far, cross_near, cross_far, corner_far,
    out_near, main_far, out_far, grid_ref,
):
    half, columns = own_near.shape[:2]
    rows = 2 * half
    wide = columns + 4
    p, q = parities(info_ref)
    near_row, far_row = (rows + 2) * (1 - p), (rows + 2) * p
    near_column, far_column = (columns + 2) * (1 - q), (columns + 2) * q
    for source, start in (
        (own_near, 2 + half * (1 - p)), (own_far, 2 + half * p),
        (got_near, near_row), (got_far, far_row),
    ):
        for i in range(2):
            for j in range(columns):
                grid_ref[(start + i) * wide + 2 + j] = source[i, j]
    for source, start in ((cross_near, near_column), (cross_far, far_column)):
        for i in range(rows):
            for j in range(2):
                grid_ref[(2 + i) * wide + start + j] = source[i, j]
    for source, start, first in ((got_near, near_row, columns), (corner_far, far_row, 0)):
        for i in range(2):
            for j in range(2):
                grid_ref[(start + i) * wide + near_column + j] = source[i, first + j]
                grid_ref[(start + i) * wide + far_column + j] = source[i, first + 2 + j]
    for main, corner, first, start in (
        (main_far, out_far, 0, far_row), (out_near, out_near, columns, near_row)
    ):
        for i in range(2):
            base = (start + i) * wide
            for j in range(2):
                corner[i, first + j] = fix_of(
                    pattern_ref, blocks_ref, grid_ref, base + near_column + j
                )
                corner[i, first + 2 + j] = fix_of(
                    pattern_ref, blocks_ref, grid_ref, base + far_column + j
                )
            for j in range(columns):
                main[i, j] = fix_of(pattern_ref, blocks_ref, grid_ref, base + 2 + j)


def margin_fixes(info, pattern, blocks, pieces):
    count, width, depth = blocks.shape
    half, columns, _, sides = pieces[0].shape
    near = shaped((2, columns + 4, width, sides), BF16)
    main = shaped((2, columns, width, sides), BF16)
    corner = shaped((2, 4, width, sides), BF16)
    grid = shaped((count, width, sides), BF16)
    return call(
        margin_kernel, "margin_fixes", (near, main, corner, grid),
        (info, pattern, blocks) + pieces, [SMEM, SMEM] + [VMEM] * 8, (VMEM,) * 4, 12,
    )


def center_kernel(info_ref, pattern_ref, blocks_ref, grid_ref, side_near, side_far, center_ref):
    rows, columns = center_ref.shape[:2]
    wide = columns + 4
    _, q = parities(info_ref)
    near_column, far_column = (columns + 2) * (1 - q), (columns + 2) * q
    for i in range(rows):
        base = (2 + i) * wide
        for j in range(2):
            side_near[i, j] = fix_of(pattern_ref, blocks_ref, grid_ref, base + near_column + j)
            side_far[i, j] = fix_of(pattern_ref, blocks_ref, grid_ref, base + far_column + j)
        for j in range(columns):
            center_ref[i, j] = fix_of(pattern_ref, blocks_ref, grid_ref, base + 2 + j)


def center_fixes(info, pattern, blocks, grid, rows, columns):
    _, width, sides = grid.shape
    side = shaped((rows, 2, width, sides), BF16)
    return call(
        center_kernel, "center_fixes",
        (side, side, shaped((rows, columns, width, sides), BF16)),
        (info, pattern, blocks, grid), [SMEM, SMEM, VMEM, VMEM], (VMEM,) * 3, 12, flops=0,
    )


def fold_kernel(first, info_ref, side_ref, corner_far, got_near, out_ref):
    half, wide = got_near.shape[:2]
    p, _ = parities(info_ref)
    for source, start, base in ((got_near, half * (1 - p), wide - 4), (corner_far, half * p, 0)):
        for i in range(half):
            for j in range(2):
                total = side_ref[start + i, j].astype(F32)
                total = total + source[i, base + first + j].astype(F32)
                out_ref[start + i, j] = total.astype(BF16)


def fold_side(first, info, side, corner_far, got_near):
    def kernel(*refs):
        fold_kernel(first, *refs)

    return call(
        kernel, "fold_side", shaped(side.shape, BF16), (info, side, corner_far, got_near),
        [SMEM] + [VMEM] * 3, VMEM, 3,
    )


def split_dot(left, right):
    high = right.astype(BF16)
    low = (right - high.astype(F32)).astype(BF16)
    return jnp.dot(left, high, preferred_element_type=F32) + jnp.dot(
        left, low, preferred_element_type=F32
    )


def solve_kernel(bits, info_ref, agg_ref, first_ref, second_ref, out_ref, sums, coarse):
    count, height, sides = first_ref.shape
    rows, columns = agg_ref.shape
    fields = rows * columns * 4
    size = height - fields
    total = sums.shape[0]
    row = lax.broadcasted_iota(jnp.int32, (sides, fields), 0)
    column = lax.broadcasted_iota(jnp.int32, (sides, fields), 1)
    repeat = jnp.where(row - 3 * size == column // 4, 1.0, 0.0).astype(BF16)
    row = lax.broadcasted_iota(jnp.int32, (total, fields), 0)
    column = lax.broadcasted_iota(jnp.int32, (total, fields), 1)
    same_field = row % 4 == column % 4
    owner = (row // 4).astype(F32)
    for part, source in enumerate((first_ref, second_ref)):
        for k in range(count):
            tail = source[k, pl.ds(fields, 16), :]
            labels = jnp.dot(tail, repeat, preferred_element_type=F32)[:1]
            onehot = jnp.where(same_field & (owner == labels), 1.0, 0.0).astype(BF16)
            found = jnp.dot(
                onehot, source[k, pl.ds(0, fields), :], preferred_element_type=F32
            )
            if part == 0 and k == 0:
                sums[...] = found
            else:
                sums[...] += found
    for part, source in enumerate((first_ref, second_ref)):
        for k in range(count):
            slot, flips = part * count + k, 0
            for i, bit in enumerate(bits):
                if slot >> i & 1:
                    flips |= bit
            start = pl.multiple_of((info_ref[1] ^ flips) * size, size)
            mine = sums[pl.ds(start, size), :]
            stacked = jnp.concatenate([mine, mine, mine, jnp.zeros_like(mine)], axis=0)
            coarse[pl.ds(start, size), :] = split_dot(
                source[k, pl.ds(fields, size), :], stacked
            )
    row = lax.broadcasted_iota(jnp.int32, (fields, 1), 0)
    labels = jnp.zeros((fields, 1), jnp.int32)
    for i in range(rows):
        for j in range(columns):
            labels = jnp.where(row // 4 == i * columns + j, agg_ref[i, j], labels)
    row = lax.broadcasted_iota(jnp.int32, (fields, total), 0)
    column = lax.broadcasted_iota(jnp.int32, (fields, total), 1)
    onehot = jnp.where((column // 4 == labels) & (column % 4 == row % 4), 1.0, 0.0)
    out_ref[...] = split_dot(onehot.astype(BF16), coarse[...])


def coarse_values(bits, info, agg, first, second):
    count, height, sides = first.shape
    fields = agg.size * 4
    total = 2 * count * (height - fields)

    def kernel(*refs):
        solve_kernel(bits, *refs)

    return call(
        kernel, "coarse_values", shaped((fields, sides), F32), (info, agg, first, second),
        [SMEM, SMEM, VMEM, VMEM], VMEM, 8,
        scratch=[pltpu.VMEM((total, sides), F32), pltpu.VMEM((total, sides), F32)],
    )


def join_kernel(
    info_ref, lifted_ref, center_ref, main_near, main_far, cross_far, cross_near, out_ref
):
    rows, columns, width, sides = center_ref.shape
    half = rows // 2
    cells = width // 4
    p, q = parities(info_ref)
    for i in range(rows):
        for j in range(columns):
            block = i * columns + j
            lifted = jnp.concatenate(
                [
                    jnp.broadcast_to(lifted_ref[pl.ds(block * 4 + f, 1), :], (cells, sides))
                    for f in range(4)
                ],
                axis=0,
            )
            out_ref[i, j] = center_ref[i, j].astype(F32) + lifted
    for source, start in ((main_near, half * (1 - p)), (main_far, half * p)):
        for i in range(half):
            for j in range(columns):
                out_ref[start + i, j] += source[i, j].astype(F32)
    for source, start in ((cross_near, (columns - 2) * (1 - q)), (cross_far, (columns - 2) * q)):
        for i in range(rows):
            for j in range(2):
                out_ref[i, start + j] += source[i, j].astype(F32)
    for i in range(rows):
        for j in range(columns):

            @pl.when(i * columns + j >= info_ref[0])
            def _(i=i, j=j):
                out_ref[i, j] = jnp.zeros((width, sides), F32)


def join(info, lifted, center, main_near, main_far, cross_far, cross_near):
    return call(
        join_kernel, "join", shaped(center.shape, F32),
        (info, lifted, center, main_near, main_far, cross_far, cross_near),
        [SMEM] + [VMEM] * 6, VMEM, 6,
    )


def body(residual, approx_inverse, pattern, live_blocks, block_aggregate, coarse_inverse):
    rows, columns = residual.shape[:2]
    info = jnp.stack([live_blocks[0, 0], lax.axis_index("stream"), lax.axis_index("cross")])
    own_near, own_far, edge_near, edge_far = mask_blocks(info, residual)
    bits = []
    while 2 << len(bits) <= lax.axis_size("stream"):
        bits.insert(0, 1 << len(bits))
    gathered = payload_of(info, block_aggregate, own_near, own_far, coarse_inverse)
    got_far = swap_far(own_far, "stream")
    cross_far = swap_far(edge_far, "cross")
    cross_near = swap_near(edge_near, "cross")
    blocks, links = approx_inverse[0], jnp.transpose(pattern[0])
    got_far, cross_far, cross_near, gathered = lax.optimization_barrier(
        (got_far, cross_far, cross_near, gathered)
    )
    other = swap_bit(gathered, "stream", bits[0])
    got_near, corner_far = corners(info, own_near, cross_near, cross_far)
    corner_far = swap_far(corner_far, "stream")
    got_near = swap_near(got_near, "stream")
    gathered = join_pair(gathered, other)
    other = swap_bit(gathered, "stream", bits[1])
    gathered, corner_far, got_near = lax.optimization_barrier((gathered, corner_far, got_near))
    pieces = (own_near, own_far, got_near, got_far, cross_near, cross_far, corner_far)
    near, far, corner_far, grid = margin_fixes(info, links, blocks, pieces)
    corner_far, other = lax.optimization_barrier((corner_far, other))
    corner_far = swap_far(corner_far, "stream")
    near = swap_near(near, "stream")
    far = swap_far(far, "stream")
    if bits[2:]:
        gathered = join_pair(gathered, other)
        other = swap_bit(gathered, "stream", bits[2])
    near, grid = lax.optimization_barrier((near, grid))
    side_near, side_far, center = center_fixes(info, links, blocks, grid, rows, columns)
    side_near, other = lax.optimization_barrier((side_near, other))
    for bit in bits[3:]:
        gathered = join_pair(gathered, other)
        other = swap_bit(gathered, "stream", bit)
    gathered, near, corner_far = lax.optimization_barrier((gathered, near, corner_far))
    side_far = fold_side(2, info, side_far, corner_far, near)
    side_far, side_near = lax.optimization_barrier((side_far, side_near))
    side_near = fold_side(0, info, side_near, corner_far, near)
    cross_far = swap_far(side_far, "cross")
    cross_near = swap_near(side_near, "cross")
    lifted = coarse_values(bits, info, block_aggregate, gathered, other)
    return join(info, lifted, center, near, far, cross_far, cross_near)


def solution(mesh):
    placed = (
        P("stream", "cross", None, None),
        P("stream", "cross", None, None),
        P("stream", "cross", None),
        P("stream", "cross"),
        P("stream", "cross"),
        P("stream", "cross"),
    )
    return jax.shard_map(
        body,
        mesh=mesh,
        in_specs=placed,
        out_specs=P("stream", "cross", None, None),
        check_vma=False,
    )
```
